32 devices in a mesh: sample: 4 (over z), row: 2 (over y), col: 4 (over x, core).
Axes of the slice: x: 2, y: 2, z: 4, core: 2. Of those that a mesh axis runs over, the one named last changes fastest.
Arguments:
- single: bfloat16 [2048, 384], P(('sample', 'row')), parts along dimension 0, may hold values from -16 to 16
- pair_bias: bfloat16 [64, 512, 512], P('sample', 'row', 'col'), parts along dimension 0, may hold values from -4 to 400
- token_mask: int32 [2048], P('sample'), parts along dimension 0, may hold values from 0 to 1, as said below
- norm_gain: float32 [384], replicated, may hold values from 0.25 to 1.75
- w_query: bfloat16 [384, 384], replicated, may hold values from -0.3125 to 0.3125
- query_bias: float32 [384], replicated, may hold values from -3 to 3
- w_key: bfloat16 [384, 384], replicated, may hold values from -0.3125 to 0.3125
- w_value: bfloat16 [384, 384], replicated, may hold values from -0.3125 to 0.3125
- w_gate: bfloat16 [384, 384], replicated, may hold values from -0.3125 to 0.3125
- w_out: bfloat16 [384, 384], P(None, 'col'), may hold values from -0.3125 to 0.3125
Outputs:
- updated: float32 [2048, 384], P(('sample', 'row'), 'col'), parts along dimension 0
The draws below stay inside these ranges and needn't reach their ends.
There are 4 independent parts, one for each index of `sample`. The reference program is written for one: setup_inputs(seed, part) draws one part's arguments, and reference() takes and returns one part's arrays. A program takes and returns all parts, laid end to end along the dimension named above; an argument that names none is the same for every part. Nothing has to cross between parts.
Inputs may be any that keep to these rules, and one draw needn't show every extreme that they name: `token_mask`: 1 for a leading run of 64 or more tokens and 0 for every token after it.
All inputs are finite; a program needn't handle non-finite values.
Results may differ from the reference program's by a relative error of at most 0.0014.
Values may be sent and summed in bfloat16 or wider, within the bound.
No kernel may reach another device: no remote copies, remote signals or barrier semaphores. Data moves between devices by JAX's collectives and lax.ppermute only.
A program may use at most 128 MiB of HBM per device.

```python
import math
import jax
import jax.numpy as jnp
from jax import lax

D = 384
HEADS = 16
TOKENS = 512


def draw_single(key, part):
    result = jnp.clip(jax.random.normal(key, (TOKENS, D), jnp.float32), -4.0, 4.0)
    return result.astype(jnp.bfloat16)


def draw_pair_bias(key, part):
    shape = (HEADS, TOKENS, TOKENS)
    result = jnp.clip(jax.random.normal(key, shape, jnp.float32), -4.0, 4.0)
    return result.astype(jnp.bfloat16)


def draw_token_mask(key, part):
    length = jax.random.randint(key, (), TOKENS // 8, TOKENS)
    return (jnp.arange(TOKENS, dtype=jnp.int32) < length).astype(jnp.int32)


def level_of(own_key, extent, pieces, low, largest):
    def one(position, shards_of):
        steps = jax.random.uniform(jax.random.fold_in(jax.random.fold_in(own_key, 6), position), (shards_of,), jnp.float32, low / len(pieces), largest / len(pieces))
        return jnp.repeat(jnp.exp(steps), extent[position] // shards_of).reshape((-1,) + (1,) * (len(extent) - position - 1))

    loudness = one(*pieces[0])
    for cut in pieces[1:]:
        loudness = loudness * one(*cut)
    return loudness


def bell_draw(key, dims, deviation, reach, cuts=(), kind=jnp.bfloat16):
    loudness = level_of(key, dims, cuts, -0.22, 0.18) if cuts else 1.0
    array = jax.random.normal(key, dims, jnp.float32) * deviation * loudness
    return jnp.minimum(jnp.maximum(array, -reach), reach).astype(kind)


def setup_inputs(seed: int = 0, part: int = 0) -> dict:
    key_of = jax.random.split(jax.random.key(seed), 11)
    own_keys = jax.random.split(jax.random.fold_in(key_of[10], part), 11)
    single = draw_single(jax.random.fold_in(jax.random.fold_in(key_of[10], part), 71), part)
    pair_bias = draw_pair_bias(jax.random.fold_in(jax.random.fold_in(key_of[10], part), 71), part)
    token_mask = draw_token_mask(jax.random.fold_in(jax.random.fold_in(key_of[10], part), 71), part)
    norm_gain = jnp.clip(1.0 + 0.15 * jax.random.normal(key_of[3], (D,), jnp.float32), 0.25, 1.75)
    w_query = bell_draw(key_of[4], (D, D), D ** -0.5, 0.3125)
    query_bias = bell_draw(key_of[5], (D,), 0.5, 3.0, (), jnp.float32)
    w_key = bell_draw(key_of[6], (D, D), D ** -0.5, 0.3125)
    w_value = bell_draw(key_of[7], (D, D), D ** -0.5, 0.3125)
    w_gate = bell_draw(key_of[8], (D, D), D ** -0.5, 0.3125)
    w_out = bell_draw(key_of[9], (D, D), D ** -0.5, 0.3125, ((1, 4),))
    return {"single": single, "pair_bias": pair_bias, "token_mask": token_mask, "norm_gain": norm_gain, "w_query": w_query, "query_bias": query_bias, "w_key": w_key, "w_value": w_value, "w_gate": w_gate, "w_out": w_out}


def layer_norm(single, norm_gain):
    values_f32 = single.astype(jnp.float32)
    row_mean = lax.optimization_barrier(jnp.mean(values_f32, axis=1, keepdims=True))
    centered = values_f32 - row_mean
    row_var = lax.optimization_barrier(jnp.mean(centered * centered, axis=1, keepdims=True))
    return (centered * lax.rsqrt(row_var + 1e-05) * norm_gain).astype(jnp.bfloat16)

def reference(single, pair_bias, token_mask, norm_gain, w_query, query_bias, w_key, w_value, w_gate, w_out):
    head_dim = D // HEADS
    inv_sqrt = 1.0 / math.sqrt(head_dim)
    normed = layer_norm(single, norm_gain)
    query = ((jnp.dot(normed, w_query, preferred_element_type=jnp.float32) + query_bias) * inv_sqrt).astype(jnp.bfloat16)
    key_rows = jnp.dot(normed, w_key, preferred_element_type=jnp.float32).astype(jnp.bfloat16)
    value_rows = jnp.dot(normed, w_value, preferred_element_type=jnp.float32).astype(jnp.bfloat16)
    gate_act = jax.nn.sigmoid(jnp.dot(normed, w_gate, preferred_element_type=jnp.float32))
    mask_term = (token_mask.astype(jnp.float32) - 1.0) * 1000000.0
    query_heads = query.reshape(TOKENS, HEADS, head_dim).transpose(1, 0, 2)
    key_heads = key_rows.reshape(TOKENS, HEADS, head_dim).transpose(1, 0, 2)
    value_heads = value_rows.reshape(TOKENS, HEADS, head_dim).transpose(1, 0, 2)

    def one_head(packed):
        query_h, key_h, value_h, bias_h = packed
        logits = jnp.dot(query_h, key_h.T, preferred_element_type=jnp.float32)
        logits = logits + bias_h.astype(jnp.float32) + mask_term[None, :]
        row_peak = lax.optimization_barrier(jnp.max(logits, axis=1, keepdims=True))
        exp_scores = jnp.exp(logits - row_peak)
        row_total = lax.optimization_barrier(jnp.sum(exp_scores, axis=1, keepdims=True))
        weighted = jnp.dot(exp_scores.astype(jnp.bfloat16), value_h, preferred_element_type=jnp.float32)
        return weighted / row_total
    attended = lax.map(one_head, (query_heads, key_heads, value_heads, pair_bias))
    attended = attended.transpose(1, 0, 2).reshape(TOKENS, D)
    gated = (gate_act * attended).astype(jnp.bfloat16)
    return single.astype(jnp.float32) + jnp.dot(gated, w_out, preferred_element_type=jnp.float32)
```

```python
import functools
import math

import jax
import jax.numpy as jnp
from jax import lax
from jax.experimental import pallas as pl
from jax.experimental.pallas import tpu as pltpu
from jax.sharding import PartitionSpec as P

D = 384
HEADS = 16
EPS = 1e-05
HEAD_DIM = D // HEADS
SCALE = 1.0 / math.sqrt(HEAD_DIM)
NT = (((1,), (1,)), ((), ()))
F32 = jnp.float32
BF16 = jnp.bfloat16


def layer_norm(single, norm_gain):
    values_f32 = single.astype(jnp.float32)
    row_mean = jnp.mean(values_f32, axis=1, keepdims=True)
    centered = values_f32 - row_mean
    row_var = jnp.mean(centered * centered, axis=1, keepdims=True)
    return (centered * lax.rsqrt(row_var + EPS) * norm_gain).astype(jnp.bfloat16)


def attend(query_rows, key_rows, value_rows, bias_block, mask_cols):
    row_count = query_rows.shape[0]
    col_count = key_rows.shape[0]
    query_heads = query_rows.reshape(row_count, HEADS, -1)
    key_heads = key_rows.reshape(col_count, HEADS, -1)
    value_heads = value_rows.reshape(col_count, HEADS, -1)
    logits = jnp.einsum("qhd,khd->hqk", query_heads, key_heads, preferred_element_type=jnp.float32)
    mask_term = (mask_cols.astype(jnp.float32) - 1.0) * 1000000.0
    logits = logits + bias_block.astype(jnp.float32) + mask_term[None, None, :]
    row_peak = jnp.max(logits, axis=2)
    exp_scores = jnp.exp(logits - row_peak[:, :, None])
    row_total = jnp.sum(exp_scores, axis=2)
    weighted = jnp.einsum(
        "hqk,khd->qhd",
        exp_scores.astype(jnp.bfloat16),
        value_heads,
        preferred_element_type=jnp.float32,
    )
    return (row_total.T, weighted.reshape(row_count, -1))


def general_plan(
    single, pair_bias, token_mask, norm_gain, w_query, query_bias, w_key, w_value, w_gate, w_out
):
    tok_rows = single.shape[0]
    col_total = lax.axis_size("col")
    out_width = w_out.shape[1]
    col_pos = lax.axis_index("col")
    normed = layer_norm(single, norm_gain)
    query = (
        (jnp.dot(normed, w_query, preferred_element_type=jnp.float32) + query_bias) * SCALE
    ).astype(jnp.bfloat16)
    gate_act = jax.nn.sigmoid(jnp.dot(normed, w_gate, preferred_element_type=jnp.float32))
    single_cols = lax.dynamic_slice_in_dim(single, col_pos * out_width, out_width, 1).astype(
        jnp.float32
    )
    key_local = jnp.dot(normed, w_key, preferred_element_type=jnp.float32).astype(jnp.bfloat16)
    value_local = jnp.dot(normed, w_value, preferred_element_type=jnp.float32).astype(jnp.bfloat16)
    key_rows = lax.all_gather(key_local, "row", axis=0, tiled=True)
    value_rows = lax.all_gather(value_local, "row", axis=0, tiled=True)
    sub_rows = tok_rows // col_total
    query_start = col_pos * sub_rows
    bias_panel = lax.all_to_all(pair_bias, "col", split_axis=1, concat_axis=2, tiled=True)
    query_part = lax.dynamic_slice_in_dim(query, query_start, sub_rows, 0)
    gate_part = lax.dynamic_slice_in_dim(gate_act, query_start, sub_rows, 0)
    row_total, weighted = attend(query_part, key_rows, value_rows, bias_panel, token_mask)
    attended = weighted / jnp.repeat(row_total, HEAD_DIM, axis=1)
    gated_part = (gate_part * attended).astype(jnp.bfloat16)
    gated_all = lax.all_gather(gated_part, "col", axis=0, tiled=True)
    return single_cols + jnp.dot(gated_all, w_out, preferred_element_type=jnp.float32)


def place():
    col = lax.axis_index("col")
    row = lax.axis_index("row")
    chip = col // 2
    core = col % 2
    half = (chip + core) % 2
    return row, col, chip, core, half


def prepare_kernel(
    single_ref, gain_ref, wq_ref, bq_ref, wk_ref, wv_ref, wg_ref, wo_ref,
    q_ref, gate_ref, wkv_ref, wo_own_ref, wo_oth_ref, res_ref, tmp_ref,
):
    _, col, _, _, half = place()
    hd = D // 2
    width = wo_ref.shape[0]
    x = single_ref[...].astype(F32)
    normed = layer_norm(single_ref[...], gain_ref[...])
    query = (jnp.dot(normed, wq_ref[...], preferred_element_type=F32) + bq_ref[...]) * SCALE
    q_ref[...] = jnp.where(half == 0, query[:, :hd], query[:, hd:]).astype(BF16)
    n = x.shape[0]
    gate = jnp.dot(normed, wg_ref[...], preferred_element_type=F32)
    tmp_ref[:, :n] = gate.T
    gate_ref[...] = jax.nn.sigmoid(tmp_ref[pl.ds(pl.multiple_of(half * hd, 8), hd), :n])
    tmp_ref[:, :n] = x.T
    res_ref[...] = tmp_ref[pl.ds(pl.multiple_of(col * width, 8), width), :n]
    tmp_ref[...] = wk_ref[...].astype(F32).T
    wkv_ref[:hd, :] = tmp_ref[pl.ds(pl.multiple_of(half * hd, 8), hd), :].astype(BF16)
    tmp_ref[...] = wv_ref[...].astype(F32).T
    wkv_ref[hd:, :] = tmp_ref[pl.ds(pl.multiple_of(half * hd, 8), hd), :].astype(BF16)
    wo = wo_ref[...].astype(F32)
    wo_own_ref[...] = jnp.where(half == 0, wo[:, :hd], wo[:, hd:]).astype(BF16)
    wo_oth_ref[...] = jnp.where(half == 0, wo[:, hd:], wo[:, :hd]).astype(BF16)


def partial_kernel(
    recv_ref, own_ref, gain_ref, wkv_ref, q_ref, bias_ref, bias_in_ref, mask_ref,
    send_ref, att_ref, lse_ref, kv_ref,
):
    row, _, chip, core, half = place()
    hd = D // 2
    heads = HEADS // 2
    n_q = q_ref.shape[0]
    n_k = recv_ref.shape[0]
    blk = n_k // 2
    first = pl.multiple_of(core * blk, blk)
    second = pl.multiple_of((1 - core) * blk, blk)

    @pl.when(chip == row)
    def _():
        kv_ref[:blk, :] = own_ref[pl.ds(first, blk), :]
        kv_ref[blk:, :] = own_ref[pl.ds(second, blk), :]

    @pl.when(chip != row)
    def _():
        kv_ref[:blk, :] = recv_ref[pl.ds(first, blk), :]
        kv_ref[blk:, :] = recv_ref[pl.ds(second, blk), :]

    base = chip * n_k
    mask_a = mask_ref[:, pl.ds(pl.multiple_of(base + first, blk), blk)]
    mask_b = mask_ref[:, pl.ds(pl.multiple_of(base + second, blk), blk)]
    mask_a = (mask_a.astype(F32) - 1.0) * 1000000.0
    mask_b = (mask_b.astype(F32) - 1.0) * 1000000.0
    normed = layer_norm(kv_ref[...], gain_ref[...])
    kv_t = lax.dot_general(wkv_ref[...], normed, NT, preferred_element_type=F32)
    key_t = kv_t[:hd].astype(BF16)
    query = q_ref[...]
    feature = lax.broadcasted_iota(jnp.int32, (1, hd), 1)
    lane = lax.broadcasted_iota(jnp.int32, (n_q, 128), 1)
    peaks = jnp.zeros((n_q, 128), F32)
    ones = jnp.ones((8, n_k), F32)
    sums = []
    for h in range(heads):
        lo = h * HEAD_DIM
        own_feat = ((feature >= lo) & (feature < lo + HEAD_DIM)).astype(F32).astype(BF16)
        logits = jnp.dot(query * own_feat, key_t, preferred_element_type=F32)
        la = logits[:, :blk] + bias_ref[half * heads + h].astype(F32) + mask_a
        lb = logits[:, blk:] + bias_in_ref[h].astype(F32) + mask_b
        peak = jnp.max(jnp.maximum(la, lb), axis=1, keepdims=True)
        probs = jnp.concatenate([jnp.exp(la - peak), jnp.exp(lb - peak)], axis=1).astype(BF16)
        value = jnp.concatenate([kv_t[hd + lo : hd + lo + HEAD_DIM], ones], axis=0).astype(BF16)
        out = lax.dot_general(value, probs, NT, preferred_element_type=F32)
        total = out[HEAD_DIM : HEAD_DIM + 1]
        att = out[:HEAD_DIM] / total
        att_ref[lo : lo + HEAD_DIM, :] = att
        sums.append(total)
        peaks = jnp.where(lane == h, peak, peaks)
    lse = peaks.T[:heads] + jnp.log(jnp.concatenate(sums, axis=0))
    lse_ref[...] = lse
    hi = lse.astype(BF16)
    rest = lse - hi.astype(F32)
    mid = rest.astype(BF16)
    low = (rest - mid.astype(F32)).astype(BF16)
    send_ref[:hd, :] = att_ref[...].astype(BF16)
    send_ref[hd : hd + heads, :] = hi
    send_ref[hd + heads : hd + 2 * heads, :] = mid
    send_ref[hd + 2 * heads :, :] = low


def merge_kernel(recv_ref, att_ref, lse_ref, gate_ref, gated_ref):
    hd = D // 2
    heads = HEADS // 2
    parts = recv_ref[hd:, :].astype(F32)
    other = parts[:heads] + parts[heads : 2 * heads] + parts[2 * heads :]
    own = lse_ref[...]
    top = jnp.maximum(own, other)
    w_own = jnp.exp(own - top)
    w_oth = jnp.exp(other - top)
    inv = 1.0 / (w_own + w_oth)
    w_own = w_own * inv
    w_oth = w_oth * inv
    pieces = []
    for h in range(heads):
        rows = slice(h * HEAD_DIM, (h + 1) * HEAD_DIM)
        att = w_own[h : h + 1] * att_ref[rows, :] + w_oth[h : h + 1] * recv_ref[rows, :].astype(F32)
        pieces.append(gate_ref[rows, :] * att)
    gated_ref[...] = jnp.concatenate(pieces, axis=0).astype(BF16)


def project_kernel(own_ref, oth_ref, wo_own_ref, wo_oth_ref, res_ref, out_ref):
    out_ref[...] = (
        res_ref[...]
        + jnp.dot(wo_own_ref[...], own_ref[...], preferred_element_type=F32)
        + jnp.dot(wo_oth_ref[...], oth_ref[...], preferred_element_type=F32)
    )


def call(kernel, outs, args, scratch=(), flops=0, trans=0):
    vmem = pl.BlockSpec(memory_space=pltpu.VMEM)
    nbytes = sum(math.prod(a.shape) * a.dtype.itemsize for a in (*args, *outs))
    return pl.pallas_call(
        kernel,
        out_shape=tuple(outs),
        in_specs=[vmem] * len(args),
        out_specs=tuple([vmem] * len(outs)),
        scratch_shapes=list(scratch),
        cost_estimate=pl.CostEstimate(flops=flops, bytes_accessed=nbytes, transcendentals=trans),
    )(*args)


def paired_plan(
    single, pair_bias, token_mask, norm_gain, w_query, query_bias, w_key, w_value, w_gate, w_out
):
    n = single.shape[0]
    heads, rows, cols = pair_bias.shape
    width = w_out.shape[1]
    hd = D // 2
    half_heads = heads // 2
    _, _, _, _, half = place()
    shape = jax.ShapeDtypeStruct
    swap_row = [(r * 4 + c, (1 - r) * 4 + (c ^ 1)) for r in range(2) for c in range(4)]
    swap_core = [(c, c ^ 1) for c in range(4)]
    swap_chip = [(c, c ^ 3) for c in range(4)]

    gain = norm_gain.reshape(1, D)
    single_in = lax.ppermute(single, ("row", "col"), swap_row)
    bias_out = lax.dynamic_slice_in_dim(pair_bias, (1 - half) * half_heads, half_heads, 0)
    bias_in = lax.ppermute(bias_out, "col", swap_core)
    query, gate, wkv, wo_own, wo_oth, res = call(
        prepare_kernel,
        [
            shape((n, hd), BF16),
            shape((hd, n), F32),
            shape((D, D), BF16),
            shape((width, hd), BF16),
            shape((width, hd), BF16),
            shape((width, n), F32),
        ],
        (single, gain, w_query, query_bias.reshape(1, D), w_key, w_value, w_gate, w_out.T),
        [pltpu.VMEM((D, D), F32)],
        flops=4 * n * D * D,
    )
    send, att, lse = call(
        partial_kernel,
        [
            shape((hd + 3 * half_heads, n), BF16),
            shape((hd, n), F32),
            shape((half_heads, n), F32),
        ],
        (single_in, single, gain, wkv, query, pair_bias, bias_in, token_mask.reshape(1, -1)),
        [pltpu.VMEM((n, D), BF16)],
        flops=4 * n * D * D,
        trans=half_heads * n * n,
    )
    recv = lax.ppermute(send, "col", swap_chip)
    (gated_own,) = call(merge_kernel, [shape((hd, n), BF16)], (recv, att, lse, gate), flops=n * D)
    gated_oth = lax.ppermute(gated_own, "col", swap_core)
    (out,) = call(
        project_kernel,
        [shape((width, n), F32)],
        (gated_own, gated_oth, wo_own, wo_oth, res),
        flops=2 * n * D * width,
    )
    return out.T


def on_device(single, pair_bias, *rest):
    heads, rows, cols = pair_bias.shape
    paired = (
        lax.axis_size("row") == 2
        and lax.axis_size("col") == 4
        and heads == HEADS
        and rows == single.shape[0]
        and 2 * cols == rows
        and cols % 128 == 0
    )
    plan = paired_plan if paired else general_plan
    return plan(single, pair_bias, *rest)


def solution(mesh):
    return jax.shard_map(
        on_device,
        mesh=mesh,
        in_specs=(
            P(("sample", "row"), None),
            P("sample", "row", "col"),
            P("sample"),
            P(),
            P(),
            P(),
            P(),
            P(),
            P(),
            P(None, "col"),
        ),
        out_specs=P(("sample", "row"), "col"),
        check_vma=False,
    )
```

```python
import functools
import math

import jax
import jax.numpy as jnp
from jax import lax
from jax.experimental import pallas as pl
from jax.experimental.pallas import tpu as pltpu
from jax.sharding import PartitionSpec as P

D = 384
HEADS = 16
EPS = 1e-05
HEAD_DIM = D // HEADS
SCALE = 1.0 / math.sqrt(HEAD_DIM)
NT = (((1,), (1,)), ((), ()))
F32 = jnp.float32
BF16 = jnp.bfloat16


def layer_norm(single, norm_gain):
    values_f32 = single.astype(jnp.float32)
    row_mean = jnp.mean(values_f32, axis=1, keepdims=True)
    centered = values_f32 - row_mean
    row_var = jnp.mean(centered * centered, axis=1, keepdims=True)
    return (centered * lax.rsqrt(row_var + EPS) * norm_gain).astype(jnp.bfloat16)


def attend(query_rows, key_rows, value_rows, bias_block, mask_cols):
    row_count = query_rows.shape[0]
    col_count = key_rows.shape[0]
    query_heads = query_rows.reshape(row_count, HEADS, -1)
    key_heads = key_rows.reshape(col_count, HEADS, -1)
    value_heads = value_rows.reshape(col_count, HEADS, -1)
    logits = jnp.einsum("qhd,khd->hqk", query_heads, key_heads, preferred_element_type=jnp.float32)
    mask_term = (mask_cols.astype(jnp.float32) - 1.0) * 1000000.0
    logits = logits + bias_block.astype(jnp.float32) + mask_term[None, None, :]
    row_peak = jnp.max(logits, axis=2)
    exp_scores = jnp.exp(logits - row_peak[:, :, None])
    row_total = jnp.sum(exp_scores, axis=2)
    weighted = jnp.einsum(
        "hqk,khd->qhd",
        exp_scores.astype(jnp.bfloat16),
        value_heads,
        preferred_element_type=jnp.float32,
    )
    return (row_total.T, weighted.reshape(row_count, -1))


def general_plan(
    single, pair_bias, token_mask, norm_gain, w_query, query_bias, w_key, w_value, w_gate, w_out
):
    tok_rows = single.shape[0]
    col_total = lax.axis_size("col")
    out_width = w_out.shape[1]
    col_pos = lax.axis_index("col")
    normed = layer_norm(single, norm_gain)
    query = (
        (jnp.dot(normed, w_query, preferred_element_type=jnp.float32) + query_bias) * SCALE
    ).astype(jnp.bfloat16)
    gate_act = jax.nn.sigmoid(jnp.dot(normed, w_gate, preferred_element_type=jnp.float32))
    single_cols = lax.dynamic_slice_in_dim(single, col_pos * out_width, out_width, 1).astype(
        jnp.float32
    )
    key_local = jnp.dot(normed, w_key, preferred_element_type=jnp.float32).astype(jnp.bfloat16)
    value_local = jnp.dot(normed, w_value, preferred_element_type=jnp.float32).astype(jnp.bfloat16)
    key_rows = lax.all_gather(key_local, "row", axis=0, tiled=True)
    value_rows = lax.all_gather(value_local, "row", axis=0, tiled=True)
    sub_rows = tok_rows // col_total
    query_start = col_pos * sub_rows
    bias_panel = lax.all_to_all(pair_bias, "col", split_axis=1, concat_axis=2, tiled=True)
    query_part = lax.dynamic_slice_in_dim(query, query_start, sub_rows, 0)
    gate_part = lax.dynamic_slice_in_dim(gate_act, query_start, sub_rows, 0)
    row_total, weighted = attend(query_part, key_rows, value_rows, bias_panel, token_mask)
    attended = weighted / jnp.repeat(row_total, HEAD_DIM, axis=1)
    gated_part = (gate_part * attended).astype(jnp.bfloat16)
    gated_all = lax.all_gather(gated_part, "col", axis=0, tiled=True)
    return single_cols + jnp.dot(gated_all, w_out, preferred_element_type=jnp.float32)


def place():
    col = lax.axis_index("col")
    row = lax.axis_index("row")
    chip = col // 2
    core = col % 2
    half = (chip + core) % 2
    return row, col, chip, core, half


def prepare_kernel(
    single_ref, gain_ref, wq_ref, bq_ref, wk_ref, wv_ref, wg_ref, wo_ref,
    q_ref, gate_ref, wkv_ref, wo_own_ref, wo_oth_ref, res_ref, tmp_ref,
):
    _, col, _, _, half = place()
    hd = D // 2
    width = wo_ref.shape[0]
    x = single_ref[...].astype(F32)
    normed = layer_norm(single_ref[...], gain_ref[...][None, :])
    query = (jnp.dot(normed, wq_ref[...], preferred_element_type=F32) + bq_ref[...][None, :]) * SCALE
    q_ref[...] = jnp.where(half == 0, query[:, :hd], query[:, hd:]).astype(BF16)
    n = x.shape[0]
    gate = jnp.dot(normed, wg_ref[...], preferred_element_type=F32)
    tmp_ref[:, :n] = gate.T
    gate_ref[...] = jax.nn.sigmoid(tmp_ref[pl.ds(pl.multiple_of(half * hd, 8), hd), :n])
    tmp_ref[:, :n] = x.T
    res_ref[...] = tmp_ref[pl.ds(pl.multiple_of(col * width, 8), width), :n]
    tmp_ref[...] = wk_ref[...].astype(F32).T
    wkv_ref[:hd, :] = tmp_ref[pl.ds(pl.multiple_of(half * hd, 8), hd), :].astype(BF16)
    tmp_ref[...] = wv_ref[...].astype(F32).T
    wkv_ref[hd:, :] = tmp_ref[pl.ds(pl.multiple_of(half * hd, 8), hd), :].astype(BF16)
    wo = wo_ref[...].astype(F32)
    wo_own_ref[...] = jnp.where(half == 0, wo[:, :hd], wo[:, hd:]).astype(BF16)
    wo_oth_ref[...] = jnp.where(half == 0, wo[:, hd:], wo[:, :hd]).astype(BF16)


def partial_kernel(
    recv_ref, own_ref, gain_ref, wkv_ref, q_ref, bias_ref, bias_in_ref, mask_ref,
    send_ref, att_ref, lse_ref, kv_ref,
):
    row, _, chip, core, half = place()
    hd = D // 2
    heads = HEADS // 2
    n_q = q_ref.shape[0]
    n_k = recv_ref.shape[0]
    blk = n_k // 2
    first = pl.multiple_of(core * blk, blk)
    second = pl.multiple_of((1 - core) * blk, blk)

    @pl.when(chip == row)
    def _():
        kv_ref[:blk, :] = own_ref[pl.ds(first, blk), :]
        kv_ref[blk:, :] = own_ref[pl.ds(second, blk), :]

    @pl.when(chip != row)
    def _():
        kv_ref[:blk, :] = recv_ref[pl.ds(first, blk), :]
        kv_ref[blk:, :] = recv_ref[pl.ds(second, blk), :]

    base = chip * n_k
    mask_a = mask_ref[:, pl.ds(pl.multiple_of(base + first, blk), blk)]
    mask_b = mask_ref[:, pl.ds(pl.multiple_of(base + second, blk), blk)]
    mask_a = (mask_a.astype(F32) - 1.0) * 1000000.0
    mask_b = (mask_b.astype(F32) - 1.0) * 1000000.0
    normed = layer_norm(kv_ref[...], gain_ref[...][None, :])
    kv_t = lax.dot_general(wkv_ref[...], normed, NT, preferred_element_type=F32)
    key_t = kv_t[:hd].astype(BF16)
    query = q_ref[...]
    feature = lax.broadcasted_iota(jnp.int32, (1, hd), 1)
    lane = lax.broadcasted_iota(jnp.int32, (n_q, 128), 1)
    peaks = jnp.zeros((n_q, 128), F32)
    ones = jnp.ones((8, n_k), F32)
    sums = []
    for h in range(heads):
        lo = h * HEAD_DIM
        own_feat = ((feature >= lo) & (feature < lo + HEAD_DIM)).astype(F32).astype(BF16)
        logits = jnp.dot(query * own_feat, key_t, preferred_element_type=F32)
        la = logits[:, :blk] + bias_ref[half * heads + h].astype(F32) + mask_a
        lb = logits[:, blk:] + bias_in_ref[half * heads + h].astype(F32) + mask_b
        peak = jnp.max(jnp.maximum(la, lb), axis=1, keepdims=True)
        probs = jnp.concatenate([jnp.exp(la - peak), jnp.exp(lb - peak)], axis=1).astype(BF16)
        value = jnp.concatenate([kv_t[hd + lo : hd + lo + HEAD_DIM], ones], axis=0).astype(BF16)
        out = lax.dot_general(value, probs, NT, preferred_element_type=F32)
        total = out[HEAD_DIM : HEAD_DIM + 1]
        att = out[:HEAD_DIM] / total
        att_ref[lo : lo + HEAD_DIM, :] = att
        sums.append(total)
        peaks = jnp.where(lane == h, peak, peaks)
    lse = peaks.T[:heads] + jnp.log(jnp.concatenate(sums, axis=0))
    lse_ref[...] = lse
    hi = lse.astype(BF16)
    rest = lse - hi.astype(F32)
    mid = rest.astype(BF16)
    low = (rest - mid.astype(F32)).astype(BF16)
    send_ref[:hd, :] = att_ref[...].astype(BF16)
    send_ref[hd : hd + heads, :] = hi
    send_ref[hd + heads : hd + 2 * heads, :] = mid
    send_ref[hd + 2 * heads :, :] = low


def merge_kernel(recv_ref, att_ref, lse_ref, gate_ref, gated_ref):
    hd = D // 2
    heads = HEADS // 2
    parts = recv_ref[hd:, :].astype(F32)
    other = parts[:heads] + parts[heads : 2 * heads] + parts[2 * heads :]
    own = lse_ref[...]
    top = jnp.maximum(own, other)
    w_own = jnp.exp(own - top)
    w_oth = jnp.exp(other - top)
    inv = 1.0 / (w_own + w_oth)
    w_own = w_own * inv
    w_oth = w_oth * inv
    pieces = []
    for h in range(heads):
        rows = slice(h * HEAD_DIM, (h + 1) * HEAD_DIM)
        att = w_own[h : h + 1] * att_ref[rows, :] + w_oth[h : h + 1] * recv_ref[rows, :].astype(F32)
        pieces.append(gate_ref[rows, :] * att)
    gated_ref[...] = jnp.concatenate(pieces, axis=0).astype(BF16)


def project_kernel(own_ref, oth_ref, wo_own_ref, wo_oth_ref, res_ref, out_ref):
    out_ref[...] = (
        res_ref[...]
        + jnp.dot(wo_own_ref[...], own_ref[...], preferred_element_type=F32)
        + jnp.dot(wo_oth_ref[...], oth_ref[...], preferred_element_type=F32)
    )


def call(kernel, outs, args, scratch=(), flops=0, trans=0):
    vmem = pl.BlockSpec(memory_space=pltpu.VMEM)
    nbytes = sum(math.prod(a.shape) * a.dtype.itemsize for a in (*args, *outs))
    return pl.pallas_call(
        kernel,
        out_shape=tuple(outs),
        in_specs=[vmem] * len(args),
        out_specs=tuple([vmem] * len(outs)),
        scratch_shapes=list(scratch),
        cost_estimate=pl.CostEstimate(flops=flops, bytes_accessed=nbytes, transcendentals=trans),
        compiler_params=pltpu.CompilerParams(vmem_limit_bytes=16 << 20),
    )(*args)


def paired_plan(
    single, pair_bias, token_mask, norm_gain, w_query, query_bias, w_key, w_value, w_gate, w_out
):
    n = single.shape[0]
    heads, rows, cols = pair_bias.shape
    width = w_out.shape[1]
    hd = D // 2
    half_heads = heads // 2
    shape = jax.ShapeDtypeStruct
    swap_row = [(r * 4 + c, (1 - r) * 4 + (c ^ 1)) for r in range(2) for c in range(4)]
    swap_core = [(c, c ^ 1) for c in range(4)]
    swap_chip = [(c, c ^ 3) for c in range(4)]

    gain = norm_gain
    single_in = lax.ppermute(single, ("row", "col"), swap_row)
    bias_in = lax.ppermute(pair_bias, "col", swap_core)
    query, gate, wkv, wo_own, wo_oth, res = call(
        prepare_kernel,
        [
            shape((n, hd), BF16),
            shape((hd, n), F32),
            shape((D, D), BF16),
            shape((width, hd), BF16),
            shape((width, hd), BF16),
            shape((width, n), F32),
        ],
        (single, gain, w_query, query_bias, w_key, w_value, w_gate, w_out.T),
        [pltpu.VMEM((D, D), F32)],
        flops=4 * n * D * D,
    )
    send, att, lse = call(
        partial_kernel,
        [
            shape((hd + 3 * half_heads, n), BF16),
            shape((hd, n), F32),
            shape((half_heads, n), F32),
        ],
        (single_in, single, gain, wkv, query, pair_bias, bias_in, token_mask.reshape(1, -1)),
        [pltpu.VMEM((n, D), BF16)],
        flops=4 * n * D * D,
        trans=half_heads * n * n,
    )
    recv = lax.ppermute(send, "col", swap_chip)
    (gated_own,) = call(merge_kernel, [shape((hd, n), BF16)], (recv, att, lse, gate), flops=n * D)
    gated_oth = lax.ppermute(gated_own, "col", swap_core)
    (out,) = call(
        project_kernel,
        [shape((width, n), F32)],
        (gated_own, gated_oth, wo_own, wo_oth, res),
        flops=2 * n * D * width,
    )
    return out.T


def on_device(single, pair_bias, *rest):
    heads, rows, cols = pair_bias.shape
    paired = (
        lax.axis_size("row") == 2
        and lax.axis_size("col") == 4
        and heads == HEADS
        and rows == single.shape[0]
        and 2 * cols == rows
        and cols % 128 == 0
    )
    plan = paired_plan if paired else general_plan
    return plan(single, pair_bias, *rest)


def solution(mesh):
    return jax.shard_map(
        on_device,
        mesh=mesh,
        in_specs=(
            P(("sample", "row"), None),
            P("sample", "row", "col"),
            P("sample"),
            P(),
            P(),
            P(),
            P(),
            P(),
            P(),
            P(None, "col"),
        ),
        out_specs=P(("sample", "row"), "col"),
        check_vma=False,
    )
```

```python
import functools
import math

import jax
import jax.numpy as jnp
from jax import lax
from jax.experimental import pallas as pl
from jax.experimental.pallas import tpu as pltpu
from jax.sharding import PartitionSpec as P

D = 384
HEADS = 16
EPS = 1e-05
HEAD_DIM = D // HEADS
SCALE = 1.0 / math.sqrt(HEAD_DIM)
NT = (((1,), (1,)), ((), ()))
F32 = jnp.float32
BF16 = jnp.bfloat16


def layer_norm(single, norm_gain):
    values_f32 = single.astype(jnp.float32)
    row_mean = jnp.mean(values_f32, axis=1, keepdims=True)
    centered = values_f32 - row_mean
    row_var = jnp.mean(centered * centered, axis=1, keepdims=True)
    return (centered * lax.rsqrt(row_var + EPS) * norm_gain).astype(jnp.bfloat16)


def attend(query_rows, key_rows, value_rows, bias_block, mask_cols):
    row_count = query_rows.shape[0]
    col_count = key_rows.shape[0]
    query_heads = query_rows.reshape(row_count, HEADS, -1)
    key_heads = key_rows.reshape(col_count, HEADS, -1)
    value_heads = value_rows.reshape(col_count, HEADS, -1)
    logits = jnp.einsum("qhd,khd->hqk", query_heads, key_heads, preferred_element_type=jnp.float32)
    mask_term = (mask_cols.astype(jnp.float32) - 1.0) * 1000000.0
    logits = logits + bias_block.astype(jnp.float32) + mask_term[None, None, :]
    row_peak = jnp.max(logits, axis=2)
    exp_scores = jnp.exp(logits - row_peak[:, :, None])
    row_total = jnp.sum(exp_scores, axis=2)
    weighted = jnp.einsum(
        "hqk,khd->qhd",
        exp_scores.astype(jnp.bfloat16),
        value_heads,
        preferred_element_type=jnp.float32,
    )
    return (row_total.T, weighted.reshape(row_count, -1))


def general_plan(
    single, pair_bias, token_mask, norm_gain, w_query, query_bias, w_key, w_value, w_gate, w_out
):
    tok_rows = single.shape[0]
    col_total = lax.axis_size("col")
    out_width = w_out.shape[1]
    col_pos = lax.axis_index("col")
    normed = layer_norm(single, norm_gain)
    query = (
        (jnp.dot(normed, w_query, preferred_element_type=jnp.float32) + query_bias) * SCALE
    ).astype(jnp.bfloat16)
    gate_act = jax.nn.sigmoid(jnp.dot(normed, w_gate, preferred_element_type=jnp.float32))
    single_cols = lax.dynamic_slice_in_dim(single, col_pos * out_width, out_width, 1).astype(
        jnp.float32
    )
    key_local = jnp.dot(normed, w_key, preferred_element_type=jnp.float32).astype(jnp.bfloat16)
    value_local = jnp.dot(normed, w_value, preferred_element_type=jnp.float32).astype(jnp.bfloat16)
    key_rows = lax.all_gather(key_local, "row", axis=0, tiled=True)
    value_rows = lax.all_gather(value_local, "row", axis=0, tiled=True)
    sub_rows = tok_rows // col_total
    query_start = col_pos * sub_rows
    bias_panel = lax.all_to_all(pair_bias, "col", split_axis=1, concat_axis=2, tiled=True)
    query_part = lax.dynamic_slice_in_dim(query, query_start, sub_rows, 0)
    gate_part = lax.dynamic_slice_in_dim(gate_act, query_start, sub_rows, 0)
    row_total, weighted = attend(query_part, key_rows, value_rows, bias_panel, token_mask)
    attended = weighted / jnp.repeat(row_total, HEAD_DIM, axis=1)
    gated_part = (gate_part * attended).astype(jnp.bfloat16)
    gated_all = lax.all_gather(gated_part, "col", axis=0, tiled=True)
    return single_cols + jnp.dot(gated_all, w_out, preferred_element_type=jnp.float32)


def place():
    col = lax.axis_index("col")
    row = lax.axis_index("row")
    chip = col // 2
    core = col % 2
    half = (chip + core) % 2
    return row, col, chip, core, half


def prepare_kernel(
    single_hbm, gain_hbm, mask_hbm, wq_hbm, bq_hbm, wk_hbm, wv_hbm, wg_hbm, wo_hbm,
    q_ref, gate_ref, wkv_ref, wo_own_ref, wo_oth_ref, res_ref, gain_out_ref, bar_ref,
    single_ref, gain_ref, mask_ref, wq_ref, bq_ref, wk_ref, wv_ref, wg_ref, wo_ref, tmp_ref, sems,
):
    _, col, chip, core, half = place()
    sources = (single_hbm, gain_hbm, wq_hbm, bq_hbm, wg_hbm, wk_hbm, wv_hbm, wo_hbm, mask_hbm)
    targets = (single_ref, gain_ref, wq_ref, bq_ref, wg_ref, wk_ref, wv_ref, wo_ref, mask_ref)
    copies = [
        pltpu.make_async_copy(src, dst, sems.at[i])
        for i, (src, dst) in enumerate(zip(sources, targets))
    ]
    for copy in copies:
        copy.start()
    hd = D // 2
    width = wo_ref.shape[0]
    n = single_ref.shape[0]
    blk = n // 2
    copies[0].wait()
    copies[1].wait()
    gain_out_ref[...] = gain_ref[...]
    x = single_ref[...].astype(F32)
    tmp_ref[:, :n] = x.T
    res_ref[...] = tmp_ref[pl.ds(pl.multiple_of(col * width, 8), width), :n]
    normed = layer_norm(single_ref[...], gain_ref[...][None, :])
    copies[2].wait()
    copies[3].wait()
    query = (jnp.dot(normed, wq_ref[...], preferred_element_type=F32) + bq_ref[...][None, :]) * SCALE
    q_ref[...] = jnp.where(half == 0, query[:, :hd], query[:, hd:]).astype(BF16)
    copies[4].wait()
    gate = jnp.dot(normed, wg_ref[...], preferred_element_type=F32)
    tmp_ref[:, :n] = gate.T
    gate_ref[...] = jax.nn.sigmoid(tmp_ref[pl.ds(pl.multiple_of(half * hd, 8), hd), :n])
    copies[5].wait()
    tmp_ref[...] = wk_ref[...].astype(F32).T
    wkv_ref[:hd, :] = tmp_ref[pl.ds(pl.multiple_of(half * hd, 8), hd), :].astype(BF16)
    copies[6].wait()
    tmp_ref[...] = wv_ref[...].astype(F32).T
    wkv_ref[hd:, :] = tmp_ref[pl.ds(pl.multiple_of(half * hd, 8), hd), :].astype(BF16)
    copies[7].wait()
    wo = wo_ref[...].astype(F32)
    wo_own_ref[...] = jnp.where(half == 0, wo[:, :hd], wo[:, hd:]).astype(BF16)
    wo_oth_ref[...] = jnp.where(half == 0, wo[:, hd:], wo[:, :hd]).astype(BF16)
    copies[8].wait()
    base = chip * n
    first = pl.multiple_of(base + core * blk, blk)
    second = pl.multiple_of(base + (1 - core) * blk, blk)
    bar_ref[:, :blk] = (mask_ref[:, pl.ds(first, blk)].astype(F32) - 1.0) * 1000000.0
    bar_ref[:, blk:] = (mask_ref[:, pl.ds(second, blk)].astype(F32) - 1.0) * 1000000.0


def partial_kernel(
    recv_ref, own_ref, gain_ref, wkv_ref, q_ref, bias_ref, bias_in_ref, bar_ref,
    send_ref, att_ref, lse_ref, kv_ref,
):
    row, _, chip, core, half = place()
    hd = D // 2
    heads = HEADS // 2
    n_q = q_ref.shape[0]
    n_k = recv_ref.shape[0]
    blk = n_k // 2
    first = pl.multiple_of(core * blk, blk)
    second = pl.multiple_of((1 - core) * blk, blk)

    @pl.when(chip == row)
    def _():
        kv_ref[:blk, :] = own_ref[pl.ds(first, blk), :]
        kv_ref[blk:, :] = own_ref[pl.ds(second, blk), :]

    @pl.when(chip != row)
    def _():
        kv_ref[:blk, :] = recv_ref[pl.ds(first, blk), :]
        kv_ref[blk:, :] = recv_ref[pl.ds(second, blk), :]

    mask_a = bar_ref[:, :blk]
    mask_b = bar_ref[:, blk:]
    normed = layer_norm(kv_ref[...], gain_ref[...][None, :])
    kv_t = lax.dot_general(wkv_ref[...], normed, NT, preferred_element_type=F32)
    key_t = kv_t[:hd].astype(BF16)
    query = q_ref[...]
    feature = lax.broadcasted_iota(jnp.int32, (1, hd), 1)
    lane = lax.broadcasted_iota(jnp.int32, (n_q, 128), 1)
    peaks = jnp.zeros((n_q, 128), F32)
    ones = jnp.ones((8, n_k), F32)
    sums = []
    for h in range(heads):
        lo = h * HEAD_DIM
        own_feat = ((feature >= lo) & (feature < lo + HEAD_DIM)).astype(F32).astype(BF16)
        logits = jnp.dot(query * own_feat, key_t, preferred_element_type=F32)
        la = logits[:, :blk] + bias_ref[half * heads + h].astype(F32) + mask_a
        lb = logits[:, blk:] + bias_in_ref[half * heads + h].astype(F32) + mask_b
        peak = jnp.max(jnp.maximum(la, lb), axis=1, keepdims=True)
        probs = jnp.concatenate([jnp.exp(la - peak), jnp.exp(lb - peak)], axis=1).astype(BF16)
        value = jnp.concatenate([kv_t[hd + lo : hd + lo + HEAD_DIM], ones], axis=0).astype(BF16)
        out = lax.dot_general(value, probs, NT, preferred_element_type=F32)
        total = out[HEAD_DIM : HEAD_DIM + 1]
        att = out[:HEAD_DIM] / total
        att_ref[lo : lo + HEAD_DIM, :] = att
        sums.append(total)
        peaks = jnp.where(lane == h, peak, peaks)
    lse = peaks.T[:heads] + jnp.log(jnp.concatenate(sums, axis=0))
    lse_ref[...] = lse
    hi = lse.astype(BF16)
    rest = lse - hi.astype(F32)
    mid = rest.astype(BF16)
    low = (rest - mid.astype(F32)).astype(BF16)
    send_ref[:hd, :] = att_ref[...].astype(BF16)
    send_ref[hd : hd + heads, :] = hi
    send_ref[hd + heads : hd + 2 * heads, :] = mid
    send_ref[hd + 2 * heads :, :] = low


def merge_kernel(recv_ref, att_ref, lse_ref, gate_ref, gated_ref):
    hd = D // 2
    heads = HEADS // 2
    parts = recv_ref[hd:, :].astype(F32)
    other = parts[:heads] + parts[heads : 2 * heads] + parts[2 * heads :]
    own = lse_ref[...]
    top = jnp.maximum(own, other)
    w_own = jnp.exp(own - top)
    w_oth = jnp.exp(other - top)
    inv = 1.0 / (w_own + w_oth)
    w_own = w_own * inv
    w_oth = w_oth * inv
    pieces = []
    for h in range(heads):
        rows = slice(h * HEAD_DIM, (h + 1) * HEAD_DIM)
        att = w_own[h : h + 1] * att_ref[rows, :] + w_oth[h : h + 1] * recv_ref[rows, :].astype(F32)
        pieces.append(gate_ref[rows, :] * att)
    gated_ref[...] = jnp.concatenate(pieces, axis=0).astype(BF16)


def project_kernel(own_ref, oth_ref, wo_own_ref, wo_oth_ref, res_ref, out_ref):
    out_ref[...] = (
        res_ref[...]
        + jnp.dot(wo_own_ref[...], own_ref[...], preferred_element_type=F32)
        + jnp.dot(wo_oth_ref[...], oth_ref[...], preferred_element_type=F32)
    )


def call(kernel, outs, args, scratch=(), flops=0, trans=0, fetch=False):
    vmem = pl.BlockSpec(memory_space=pltpu.VMEM)
    source = pl.BlockSpec(memory_space=pltpu.HBM) if fetch else vmem
    if fetch:
        args = [pltpu.with_memory_space_constraint(a, pltpu.HBM) for a in args]
    nbytes = sum(math.prod(a.shape) * a.dtype.itemsize for a in (*args, *outs))
    return pl.pallas_call(
        kernel,
        out_shape=tuple(outs),
        in_specs=[source] * len(args),
        out_specs=tuple([vmem] * len(outs)),
        scratch_shapes=list(scratch),
        cost_estimate=pl.CostEstimate(flops=flops, bytes_accessed=nbytes, transcendentals=trans),
        compiler_params=pltpu.CompilerParams(vmem_limit_bytes=16 << 20),
    )(*args)


def paired_plan(
    single, pair_bias, token_mask, norm_gain, w_query, query_bias, w_key, w_value, w_gate, w_out
):
    n = single.shape[0]
    heads, rows, cols = pair_bias.shape
    width = w_out.shape[1]
    hd = D // 2
    half_heads = heads // 2
    shape = jax.ShapeDtypeStruct
    swap_row = [(r * 4 + c, (1 - r) * 4 + (c ^ 1)) for r in range(2) for c in range(4)]
    swap_core = [(c, c ^ 1) for c in range(4)]
    swap_chip = [(c, c ^ 3) for c in range(4)]

    single_in = lax.ppermute(single, ("row", "col"), swap_row)
    bias_in = lax.ppermute(pair_bias, "col", swap_core)
    fetched = (
        single, norm_gain, token_mask.reshape(1, -1), w_query, query_bias, w_key, w_value, w_gate, w_out.T,
    )
    query, gate, wkv, wo_own, wo_oth, res, gain, bar = call(
        prepare_kernel,
        [
            shape((n, hd), BF16),
            shape((hd, n), F32),
            shape((D, D), BF16),
            shape((width, hd), BF16),
            shape((width, hd), BF16),
            shape((width, n), F32),
            shape((D,), F32),
            shape((1, n), F32),
        ],
        fetched,
        [
            *(pltpu.VMEM(a.shape, a.dtype) for a in fetched),
            pltpu.VMEM((D, D), F32),
            pltpu.SemaphoreType.DMA((len(fetched),)),
        ],
        flops=4 * n * D * D,
        fetch=True,
    )
    send, att, lse = call(
        partial_kernel,
        [
            shape((hd + 3 * half_heads, n), BF16),
            shape((hd, n), F32),
            shape((half_heads, n), F32),
        ],
        (single_in, single, gain, wkv, query, pair_bias, bias_in, bar),
        [pltpu.VMEM((n, D), BF16)],
        flops=4 * n * D * D,
        trans=half_heads * n * n,
    )
    recv = lax.ppermute(send, "col", swap_chip)
    (gated_own,) = call(merge_kernel, [shape((hd, n), BF16)], (recv, att, lse, gate), flops=n * D)
    gated_oth = lax.ppermute(gated_own, "col", swap_core)
    (out,) = call(
        project_kernel,
        [shape((width, n), F32)],
        (gated_own, gated_oth, wo_own, wo_oth, res),
        flops=2 * n * D * width,
    )
    return out.T


def on_device(single, pair_bias, *rest):
    heads, rows, cols = pair_bias.shape
    paired = (
        lax.axis_size("row") == 2
        and lax.axis_size("col") == 4
        and heads == HEADS
        and rows == single.shape[0]
        and 2 * cols == rows
        and cols % 128 == 0
    )
    plan = paired_plan if paired else general_plan
    return plan(single, pair_bias, *rest)


def solution(mesh):
    return jax.shard_map(
        on_device,
        mesh=mesh,
        in_specs=(
            P(("sample", "row"), None),
            P("sample", "row", "col"),
            P("sample"),
            P(),
            P(),
            P(),
            P(),
            P(),
            P(),
            P(None, "col"),
        ),
        out_specs=P(("sample", "row"), "col"),
        check_vma=False,
    )
```

```python
import math

import jax
import jax.numpy as jnp
from jax import lax
from jax.experimental import pallas as pl
from jax.experimental.pallas import tpu as pltpu
from jax.sharding import PartitionSpec as P

D = 384
HEADS = 16
EPS = 1e-05
HEAD_DIM = D // HEADS
SCALE = 1.0 / math.sqrt(HEAD_DIM)
NT = (((1,), (1,)), ((), ()))
F32 = jnp.float32
BF16 = jnp.bfloat16
PAD = 16
AHEAD = 8
CHUNK = 256
BAR_HI = -999424.0
BAR_LO = -576.0


def layer_norm(single, norm_gain):
    values_f32 = single.astype(jnp.float32)
    row_mean = jnp.mean(values_f32, axis=1, keepdims=True)
    centered = values_f32 - row_mean
    row_var = jnp.mean(centered * centered, axis=1, keepdims=True)
    return (centered * lax.rsqrt(row_var + EPS) * norm_gain).astype(jnp.bfloat16)


def attend(query_rows, key_rows, value_rows, bias_block, mask_cols):
    row_count = query_rows.shape[0]
    col_count = key_rows.shape[0]
    query_heads = query_rows.reshape(row_count, HEADS, -1)
    key_heads = key_rows.reshape(col_count, HEADS, -1)
    value_heads = value_rows.reshape(col_count, HEADS, -1)
    logits = jnp.einsum("qhd,khd->hqk", query_heads, key_heads, preferred_element_type=jnp.float32)
    mask_term = (mask_cols.astype(jnp.float32) - 1.0) * 1000000.0
    logits = logits + bias_block.astype(jnp.float32) + mask_term[None, None, :]
    row_peak = jnp.max(logits, axis=2)
    exp_scores = jnp.exp(logits - row_peak[:, :, None])
    row_total = jnp.sum(exp_scores, axis=2)
    weighted = jnp.einsum(
        "hqk,khd->qhd",
        exp_scores.astype(jnp.bfloat16),
        value_heads,
        preferred_element_type=jnp.float32,
    )
    return (row_total.T, weighted.reshape(row_count, -1))


def general_plan(
    single, pair_bias, token_mask, norm_gain, w_query, query_bias, w_key, w_value, w_gate, w_out
):
    tok_rows = single.shape[0]
    col_total = lax.axis_size("col")
    out_width = w_out.shape[1]
    col_pos = lax.axis_index("col")
    normed = layer_norm(single, norm_gain)
    query = (
        (jnp.dot(normed, w_query, preferred_element_type=jnp.float32) + query_bias) * SCALE
    ).astype(jnp.bfloat16)
    gate_act = jax.nn.sigmoid(jnp.dot(normed, w_gate, preferred_element_type=jnp.float32))
    single_cols = lax.dynamic_slice_in_dim(single, col_pos * out_width, out_width, 1).astype(
        jnp.float32
    )
    key_local = jnp.dot(normed, w_key, preferred_element_type=jnp.float32).astype(jnp.bfloat16)
    value_local = jnp.dot(normed, w_value, preferred_element_type=jnp.float32).astype(jnp.bfloat16)
    key_rows = lax.all_gather(key_local, "row", axis=0, tiled=True)
    value_rows = lax.all_gather(value_local, "row", axis=0, tiled=True)
    sub_rows = tok_rows // col_total
    query_start = col_pos * sub_rows
    bias_panel = lax.all_to_all(pair_bias, "col", split_axis=1, concat_axis=2, tiled=True)
    query_part = lax.dynamic_slice_in_dim(query, query_start, sub_rows, 0)
    gate_part = lax.dynamic_slice_in_dim(gate_act, query_start, sub_rows, 0)
    row_total, weighted = attend(query_part, key_rows, value_rows, bias_panel, token_mask)
    attended = weighted / jnp.repeat(row_total, HEAD_DIM, axis=1)
    gated_part = (gate_part * attended).astype(jnp.bfloat16)
    gated_all = lax.all_gather(gated_part, "col", axis=0, tiled=True)
    return single_cols + jnp.dot(gated_all, w_out, preferred_element_type=jnp.float32)


def place():
    col = lax.axis_index("col")
    row = lax.axis_index("row")
    chip = col // 2
    core = col % 2
    half = (chip + core) % 2
    return row, col, chip, core, half


def prepare_kernel(
    single_hbm, gain_hbm, mask_hbm, wq_hbm, bq_hbm, wk_hbm, wv_hbm, wg_hbm, wo_hbm,
    q_ref, gate_ref, wkv_ref, wo_own_ref, wo_oth_ref, res_ref, gain_out_ref, bar_ref,
    single_ref, gain_ref, mask_ref, wq_ref, bq_ref, wk_ref, wv_ref, wg_ref, wo_ref, tmp_ref, sems,
):
    _, col, chip, core, half = place()
    sources = (single_hbm, gain_hbm, wq_hbm, bq_hbm, wg_hbm, wk_hbm, wv_hbm, wo_hbm, mask_hbm)
    targets = (single_ref, gain_ref, wq_ref, bq_ref, wg_ref, wk_ref, wv_ref, wo_ref, mask_ref)
    copies = [
        pltpu.make_async_copy(src, dst, sems.at[i])
        for i, (src, dst) in enumerate(zip(sources, targets))
    ]
    for copy in copies:
        copy.start()
    hd = D // 2
    width = wo_ref.shape[0]
    n = single_ref.shape[0]
    blk = n // 2
    copies[0].wait()
    copies[1].wait()
    gain_out_ref[...] = gain_ref[...]
    x = single_ref[...].astype(F32)
    tmp_ref[:, :n] = x.T
    res_ref[...] = tmp_ref[pl.ds(pl.multiple_of(col * width, 8), width), :n]
    normed = layer_norm(single_ref[...], gain_ref[...][None, :])
    copies[2].wait()
    copies[3].wait()
    query = (jnp.dot(normed, wq_ref[...], preferred_element_type=F32) + bq_ref[...][None, :]) * SCALE
    query = jnp.where(half == 0, query[:, :hd], query[:, hd:])
    query = jnp.concatenate([query, jnp.ones((n, PAD), F32)], axis=1)
    feature = lax.broadcasted_iota(jnp.int32, query.shape, 1)
    bar_rows = (feature == hd) | (feature == hd + 1)
    for h in range(q_ref.shape[0]):
        lo = h * HEAD_DIM
        kept = ((feature >= lo) & (feature < lo + HEAD_DIM)) | bar_rows
        q_ref[h] = jnp.where(kept, query, 0.0).astype(BF16)
    copies[4].wait()
    gate = jnp.dot(normed, wg_ref[...], preferred_element_type=F32)
    tmp_ref[:, :n] = gate.T
    gate_ref[...] = jax.nn.sigmoid(tmp_ref[pl.ds(pl.multiple_of(half * hd, 8), hd), :n])
    copies[5].wait()
    tmp_ref[...] = wk_ref[...].astype(F32).T
    wkv_ref[:hd, :] = tmp_ref[pl.ds(pl.multiple_of(half * hd, 8), hd), :].astype(BF16)
    copies[6].wait()
    tmp_ref[...] = wv_ref[...].astype(F32).T
    wkv_ref[hd:, :] = tmp_ref[pl.ds(pl.multiple_of(half * hd, 8), hd), :].astype(BF16)
    copies[7].wait()
    wo = wo_ref[...].astype(F32)
    wo_own_ref[...] = jnp.where(half == 0, wo[:, :hd], wo[:, hd:]).astype(BF16)
    wo_oth_ref[...] = jnp.where(half == 0, wo[:, hd:], wo[:, :hd]).astype(BF16)
    copies[8].wait()
    base = chip * n
    first = pl.multiple_of(base + core * blk, blk)
    second = pl.multiple_of(base + (1 - core) * blk, blk)
    masked = jnp.concatenate([mask_ref[:, pl.ds(first, blk)], mask_ref[:, pl.ds(second, blk)]], axis=1)
    masked = 1.0 - masked.astype(F32)
    pad_row = lax.broadcasted_iota(jnp.int32, (PAD, n), 0)
    level = jnp.where(pad_row == 0, BAR_HI, jnp.where(pad_row == 1, BAR_LO, 0.0))
    bar_ref[...] = (level * masked).astype(BF16)


def partial_kernel(
    recv_ref, own_ref, gain_ref, wkv_ref, q_ref, bias_ref, bias_in_ref, bar_ref,
    send_ref, att_ref, lse_ref,
):
    row, _, chip, core, half = place()
    hd = D // 2
    heads = HEADS // 2
    n_q = q_ref.shape[1]
    n_k = recv_ref.shape[0]
    blk = n_k // 2
    first = pl.multiple_of(core * blk, blk)
    second = pl.multiple_of((1 - core) * blk, blk)

    local = chip == row
    block_a = jnp.where(local, own_ref[pl.ds(first, blk), :], recv_ref[pl.ds(first, blk), :])
    block_b = jnp.where(local, own_ref[pl.ds(second, blk), :], recv_ref[pl.ds(second, blk), :])
    tokens = jnp.concatenate([block_a, block_b], axis=0)
    normed = layer_norm(tokens, gain_ref[...][None, :])
    kv_t = lax.dot_general(wkv_ref[...], normed, NT, preferred_element_type=F32)
    key_t = jnp.concatenate([kv_t[:hd].astype(BF16), bar_ref[...]], axis=0)
    lane = lax.broadcasted_iota(jnp.int32, (n_q, 128), 1)
    peaks = jnp.zeros((n_q, 128), F32)
    ones = jnp.ones((8, n_k), F32)
    sums = []

    def logits_of(task):
        h, start = task
        return jnp.dot(q_ref[h, start : start + CHUNK, :], key_t, preferred_element_type=F32)

    tasks = [(h, start) for h in range(heads) for start in range(0, n_q, CHUNK)]
    ready = [logits_of(task) for task in tasks[:AHEAD]]
    probs, tops = [], []
    for i, (h, start) in enumerate(tasks):
        lo = h * HEAD_DIM
        rows = slice(start, start + CHUNK)
        logits = ready.pop(0)
        if i + AHEAD < len(tasks):
            ready.append(logits_of(tasks[i + AHEAD]))
        la = logits[:, :blk] + bias_ref[half * heads + h, rows, :].astype(F32)
        lb = logits[:, blk:] + bias_in_ref[half * heads + h, rows, :].astype(F32)
        peak = jnp.max(jnp.maximum(la, lb), axis=1, keepdims=True)
        probs.append(jnp.concatenate([jnp.exp(la - peak), jnp.exp(lb - peak)], axis=1).astype(BF16))
        tops.append(peak)
        if start + CHUNK < n_q:
            continue
        value = jnp.concatenate([kv_t[hd + lo : hd + lo + HEAD_DIM], ones], axis=0).astype(BF16)
        out = lax.dot_general(
            value, jnp.concatenate(probs, axis=0), NT, preferred_element_type=F32
        )
        total = out[HEAD_DIM : HEAD_DIM + 1]
        att_ref[lo : lo + HEAD_DIM, :] = out[:HEAD_DIM] / total
        sums.append(total)
        peaks = jnp.where(lane == h, jnp.concatenate(tops, axis=0), peaks)
        probs, tops = [], []
    lse = peaks.T[:heads] + jnp.log(jnp.concatenate(sums, axis=0))
    lse_ref[...] = lse
    hi = lse.astype(BF16)
    rest = lse - hi.astype(F32)
    mid = rest.astype(BF16)
    low = (rest - mid.astype(F32)).astype(BF16)
    send_ref[:hd, :] = att_ref[...].astype(BF16)
    send_ref[hd : hd + heads, :] = hi
    send_ref[hd + heads : hd + 2 * heads, :] = mid
    send_ref[hd + 2 * heads :, :] = low


def merge_kernel(recv_ref, att_ref, lse_ref, gate_ref, gated_ref):
    hd = D // 2
    heads = HEADS // 2
    parts = recv_ref[hd:, :].astype(F32)
    other = parts[:heads] + parts[heads : 2 * heads] + parts[2 * heads :]
    own = lse_ref[...]
    top = jnp.maximum(own, other)
    w_own = jnp.exp(own - top)
    w_oth = jnp.exp(other - top)
    inv = 1.0 / (w_own + w_oth)
    w_own = w_own * inv
    w_oth = w_oth * inv
    pieces = []
    for h in range(heads):
        rows = slice(h * HEAD_DIM, (h + 1) * HEAD_DIM)
        att = w_own[h : h + 1] * att_ref[rows, :] + w_oth[h : h + 1] * recv_ref[rows, :].astype(F32)
        pieces.append(gate_ref[rows, :] * att)
    gated_ref[...] = jnp.concatenate(pieces, axis=0).astype(BF16)


def project_kernel(own_ref, oth_ref, wo_own_ref, wo_oth_ref, res_ref, out_ref):
    out_ref[...] = (
        res_ref[...]
        + jnp.dot(wo_own_ref[...], own_ref[...], preferred_element_type=F32)
        + jnp.dot(wo_oth_ref[...], oth_ref[...], preferred_element_type=F32)
    )


def call(kernel, outs, args, scratch=(), flops=0, trans=0, fetch=False):
    vmem = pl.BlockSpec(memory_space=pltpu.VMEM)
    source = pl.BlockSpec(memory_space=pltpu.HBM) if fetch else vmem
    if fetch:
        args = [pltpu.with_memory_space_constraint(a, pltpu.HBM) for a in args]
    nbytes = sum(math.prod(a.shape) * a.dtype.itemsize for a in (*args, *outs))
    return pl.pallas_call(
        kernel,
        out_shape=tuple(outs),
        in_specs=[source] * len(args),
        out_specs=tuple([vmem] * len(outs)),
        scratch_shapes=list(scratch),
        cost_estimate=pl.CostEstimate(flops=flops, bytes_accessed=nbytes, transcendentals=trans),
        compiler_params=pltpu.CompilerParams(vmem_limit_bytes=16 << 20),
    )(*args)


def paired_plan(
    single, pair_bias, token_mask, norm_gain, w_query, query_bias, w_key, w_value, w_gate, w_out
):
    n = single.shape[0]
    heads, _, _ = pair_bias.shape
    width = w_out.shape[1]
    hd = D // 2
    half_heads = heads // 2
    shape = jax.ShapeDtypeStruct
    swap_row = [(r * 4 + c, (1 - r) * 4 + (c ^ 1)) for r in range(2) for c in range(4)]
    swap_core = [(c, c ^ 1) for c in range(4)]
    swap_chip = [(c, c ^ 3) for c in range(4)]

    single_in = lax.ppermute(single, ("row", "col"), swap_row)
    bias_in = lax.ppermute(pair_bias, "col", swap_core)
    fetched = (
        single, norm_gain, token_mask.reshape(1, -1), w_query, query_bias, w_key, w_value, w_gate, w_out.T,
    )
    query, gate, wkv, wo_own, wo_oth, res, gain, bar = call(
        prepare_kernel,
        [
            shape((half_heads, n, hd + PAD), BF16),
            shape((hd, n), F32),
            shape((D, D), BF16),
            shape((width, hd), BF16),
            shape((width, hd), BF16),
            shape((width, n), F32),
            shape((D,), F32),
            shape((PAD, n), BF16),
        ],
        fetched,
        [
            *(pltpu.VMEM(a.shape, a.dtype) for a in fetched),
            pltpu.VMEM((D, D), F32),
            pltpu.SemaphoreType.DMA((len(fetched),)),
        ],
        flops=4 * n * D * D,
        fetch=True,
    )
    send, att, lse = call(
        partial_kernel,
        [
            shape((hd + 3 * half_heads, n), BF16),
            shape((hd, n), F32),
            shape((half_heads, n), F32),
        ],
        (single_in, single, gain, wkv, query, pair_bias, bias_in, bar),
        flops=4 * n * D * D,
        trans=half_heads * n * n,
    )
    recv = lax.ppermute(send, "col", swap_chip)
    (gated_own,) = call(merge_kernel, [shape((hd, n), BF16)], (recv, att, lse, gate), flops=n * D)
    gated_oth = lax.ppermute(gated_own, "col", swap_core)
    (out,) = call(
        project_kernel,
        [shape((width, n), F32)],
        (gated_own, gated_oth, wo_own, wo_oth, res),
        flops=2 * n * D * width,
    )
    return out.T


def on_device(single, pair_bias, *rest):
    heads, rows, cols = pair_bias.shape
    paired = (
        lax.axis_size("row") == 2
        and lax.axis_size("col") == 4
        and heads == HEADS
        and rows == single.shape[0]
        and 2 * cols == rows
        and cols % 128 == 0
    )
    plan = paired_plan if paired else general_plan
    return plan(single, pair_bias, *rest)


def solution(mesh):
    return jax.shard_map(
        on_device,
        mesh=mesh,
        in_specs=(
            P(("sample", "row"), None),
            P("sample", "row", "col"),
            P("sample"),
            P(),
            P(),
            P(),
            P(),
            P(),
            P(),
            P(None, "col"),
        ),
        out_specs=P(("sample", "row"), "col"),
        check_vma=False,
    )
```

```python
import math

import jax
import jax.numpy as jnp
from jax import lax
from jax.experimental import pallas as pl
from jax.experimental.pallas import tpu as pltpu
from jax.sharding import PartitionSpec as P

D = 384
HEADS = 16
EPS = 1e-05
HEAD_DIM = D // HEADS
SCALE = 1.0 / math.sqrt(HEAD_DIM)
NT = (((1,), (1,)), ((), ()))
F32 = jnp.float32
BF16 = jnp.bfloat16
PAD = 16
AHEAD = 8
CHUNK = 256
BAR_HI = -999424.0
BAR_LO = -576.0


def layer_norm(single, norm_gain):
    values_f32 = single.astype(jnp.float32)
    row_mean = jnp.mean(values_f32, axis=1, keepdims=True)
    centered = values_f32 - row_mean
    row_var = jnp.mean(centered * centered, axis=1, keepdims=True)
    return (centered * lax.rsqrt(row_var + EPS) * norm_gain).astype(jnp.bfloat16)


def attend(query_rows, key_rows, value_rows, bias_block, mask_cols):
    row_count = query_rows.shape[0]
    col_count = key_rows.shape[0]
    query_heads = query_rows.reshape(row_count, HEADS, -1)
    key_heads = key_rows.reshape(col_count, HEADS, -1)
    value_heads = value_rows.reshape(col_count, HEADS, -1)
    logits = jnp.einsum("qhd,khd->hqk", query_heads, key_heads, preferred_element_type=jnp.float32)
    mask_term = (mask_cols.astype(jnp.float32) - 1.0) * 1000000.0
    logits = logits + bias_block.astype(jnp.float32) + mask_term[None, None, :]
    row_peak = jnp.max(logits, axis=2)
    exp_scores = jnp.exp(logits - row_peak[:, :, None])
    row_total = jnp.sum(exp_scores, axis=2)
    weighted = jnp.einsum(
        "hqk,khd->qhd",
        exp_scores.astype(jnp.bfloat16),
        value_heads,
        preferred_element_type=jnp.float32,
    )
    return (row_total.T, weighted.reshape(row_count, -1))


def general_plan(
    single, pair_bias, token_mask, norm_gain, w_query, query_bias, w_key, w_value, w_gate, w_out
):
    tok_rows = single.shape[0]
    col_total = lax.axis_size("col")
    out_width = w_out.shape[1]
    col_pos = lax.axis_index("col")
    normed = layer_norm(single, norm_gain)
    query = (
        (jnp.dot(normed, w_query, preferred_element_type=jnp.float32) + query_bias) * SCALE
    ).astype(jnp.bfloat16)
    gate_act = jax.nn.sigmoid(jnp.dot(normed, w_gate, preferred_element_type=jnp.float32))
    single_cols = lax.dynamic_slice_in_dim(single, col_pos * out_width, out_width, 1).astype(
        jnp.float32
    )
    key_local = jnp.dot(normed, w_key, preferred_element_type=jnp.float32).astype(jnp.bfloat16)
    value_local = jnp.dot(normed, w_value, preferred_element_type=jnp.float32).astype(jnp.bfloat16)
    key_rows = lax.all_gather(key_local, "row", axis=0, tiled=True)
    value_rows = lax.all_gather(value_local, "row", axis=0, tiled=True)
    sub_rows = tok_rows // col_total
    query_start = col_pos * sub_rows
    bias_panel = lax.all_to_all(pair_bias, "col", split_axis=1, concat_axis=2, tiled=True)
    query_part = lax.dynamic_slice_in_dim(query, query_start, sub_rows, 0)
    gate_part = lax.dynamic_slice_in_dim(gate_act, query_start, sub_rows, 0)
    row_total, weighted = attend(query_part, key_rows, value_rows, bias_panel, token_mask)
    attended = weighted / jnp.repeat(row_total, HEAD_DIM, axis=1)
    gated_part = (gate_part * attended).astype(jnp.bfloat16)
    gated_all = lax.all_gather(gated_part, "col", axis=0, tiled=True)
    return single_cols + jnp.dot(gated_all, w_out, preferred_element_type=jnp.float32)


def place():
    col = lax.axis_index("col")
    row = lax.axis_index("row")
    chip = col // 2
    core = col % 2
    half = (chip + core) % 2
    return row, col, chip, core, half


def pick_kernel(single_hbm, out_ref, sem):
    _, _, _, core, _ = place()
    blk = out_ref.shape[0]
    start = pl.multiple_of((1 - core) * blk, blk)
    copy = pltpu.make_async_copy(single_hbm.at[pl.ds(start, blk), :], out_ref, sem)
    copy.start()
    copy.wait()


def prepare_kernel(
    single_hbm, gain_hbm, mask_hbm, wq_hbm, bq_hbm, wk_hbm, wv_hbm, wg_hbm, wo_hbm,
    q_ref, gate_ref, wkv_ref, wo_own_ref, wo_oth_ref, res_ref, gain_out_ref, bar_ref,
    single_ref, gain_ref, mask_ref, wq_ref, bq_ref, wk_ref, wv_ref, wg_ref, wo_ref, tmp_ref, sems,
):
    _, col, chip, core, half = place()
    sources = (single_hbm, gain_hbm, wq_hbm, bq_hbm, wg_hbm, wk_hbm, wv_hbm, wo_hbm, mask_hbm)
    targets = (single_ref, gain_ref, wq_ref, bq_ref, wg_ref, wk_ref, wv_ref, wo_ref, mask_ref)
    copies = [
        pltpu.make_async_copy(src, dst, sems.at[i])
        for i, (src, dst) in enumerate(zip(sources, targets))
    ]
    for copy in copies:
        copy.start()
    hd = D // 2
    width = wo_ref.shape[0]
    n = single_ref.shape[0]
    blk = n // 2
    copies[0].wait()
    copies[1].wait()
    gain_out_ref[...] = gain_ref[...]
    x = single_ref[...].astype(F32)
    tmp_ref[:, :n] = x.T
    res_ref[...] = tmp_ref[pl.ds(pl.multiple_of(col * width, 8), width), :n]
    normed = layer_norm(single_ref[...], gain_ref[...][None, :])
    copies[2].wait()
    copies[3].wait()
    query = (jnp.dot(normed, wq_ref[...], preferred_element_type=F32) + bq_ref[...][None, :]) * SCALE
    query = jnp.where(half == 0, query[:, :hd], query[:, hd:])
    query = jnp.concatenate([query, jnp.ones((n, PAD), F32)], axis=1)
    feature = lax.broadcasted_iota(jnp.int32, query.shape, 1)
    bar_rows = (feature == hd) | (feature == hd + 1)
    for h in range(q_ref.shape[0]):
        lo = h * HEAD_DIM
        kept = ((feature >= lo) & (feature < lo + HEAD_DIM)) | bar_rows
        q_ref[h] = jnp.where(kept, query, 0.0).astype(BF16)
    copies[4].wait()
    gate = jnp.dot(normed, wg_ref[...], preferred_element_type=F32)
    tmp_ref[:, :n] = gate.T
    gate_ref[...] = jax.nn.sigmoid(tmp_ref[pl.ds(pl.multiple_of(half * hd, 8), hd), :n])
    copies[5].wait()
    tmp_ref[...] = wk_ref[...].astype(F32).T
    wkv_ref[:hd, :] = tmp_ref[pl.ds(pl.multiple_of(half * hd, 8), hd), :].astype(BF16)
    copies[6].wait()
    tmp_ref[...] = wv_ref[...].astype(F32).T
    wkv_ref[hd:, :] = tmp_ref[pl.ds(pl.multiple_of(half * hd, 8), hd), :].astype(BF16)
    copies[7].wait()
    wo = wo_ref[...].astype(F32)
    wo_own_ref[...] = jnp.where(half == 0, wo[:, :hd], wo[:, hd:]).astype(BF16)
    wo_oth_ref[...] = jnp.where(half == 0, wo[:, hd:], wo[:, :hd]).astype(BF16)
    copies[8].wait()
    base = chip * n
    first = pl.multiple_of(base + core * blk, blk)
    second = pl.multiple_of(base + (1 - core) * blk, blk)
    masked = jnp.concatenate([mask_ref[:, pl.ds(first, blk)], mask_ref[:, pl.ds(second, blk)]], axis=1)
    masked = 1.0 - masked.astype(F32)
    pad_row = lax.broadcasted_iota(jnp.int32, (PAD, n), 0)
    level = jnp.where(pad_row == 0, BAR_HI, jnp.where(pad_row == 1, BAR_LO, 0.0))
    bar_ref[...] = (level * masked).astype(BF16)


def partial_kernel(
    recv_ref, other_ref, own_ref, gain_ref, wkv_ref, q_ref, bias_ref, bias_in_ref, bar_ref,
    send_ref, att_ref, lse_ref,
):
    row, _, chip, core, half = place()
    hd = D // 2
    heads = HEADS // 2
    n_q = q_ref.shape[1]
    n_k = own_ref.shape[0]
    blk = n_k // 2
    first = pl.multiple_of(core * blk, blk)
    second = pl.multiple_of((1 - core) * blk, blk)

    local = chip == row
    block_a = jnp.where(local, own_ref[pl.ds(first, blk), :], recv_ref[...])
    block_b = jnp.where(local, own_ref[pl.ds(second, blk), :], other_ref[...])
    tokens = jnp.concatenate([block_a, block_b], axis=0)
    normed = layer_norm(tokens, gain_ref[...][None, :])
    kv_t = lax.dot_general(wkv_ref[...], normed, NT, preferred_element_type=F32)
    key_t = jnp.concatenate([kv_t[:hd].astype(BF16), bar_ref[...]], axis=0)
    lane = lax.broadcasted_iota(jnp.int32, (n_q, 128), 1)
    peaks = jnp.zeros((n_q, 128), F32)
    ones = jnp.ones((8, n_k), F32)
    sums = []

    def logits_of(task):
        h, start = task
        return jnp.dot(q_ref[h, start : start + CHUNK, :], key_t, preferred_element_type=F32)

    tasks = [(h, start) for h in range(heads) for start in range(0, n_q, CHUNK)]
    ready = [logits_of(task) for task in tasks[:AHEAD]]
    probs, tops = [], []
    for i, (h, start) in enumerate(tasks):
        lo = h * HEAD_DIM
        rows = slice(start, start + CHUNK)
        logits = ready.pop(0)
        if i + AHEAD < len(tasks):
            ready.append(logits_of(tasks[i + AHEAD]))
        la = logits[:, :blk] + bias_ref[half * heads + h, rows, :].astype(F32)
        lb = logits[:, blk:] + bias_in_ref[half * heads + h, rows, :].astype(F32)
        peak = jnp.max(jnp.maximum(la, lb), axis=1, keepdims=True)
        probs.append(jnp.concatenate([jnp.exp(la - peak), jnp.exp(lb - peak)], axis=1).astype(BF16))
        tops.append(peak)
        if start + CHUNK < n_q:
            continue
        value = jnp.concatenate([kv_t[hd + lo : hd + lo + HEAD_DIM], ones], axis=0).astype(BF16)
        out = lax.dot_general(
            value, jnp.concatenate(probs, axis=0), NT, preferred_element_type=F32
        )
        total = out[HEAD_DIM : HEAD_DIM + 1]
        att_ref[lo : lo + HEAD_DIM, :] = out[:HEAD_DIM] / total
        sums.append(total)
        peaks = jnp.where(lane == h, jnp.concatenate(tops, axis=0), peaks)
        probs, tops = [], []
    lse = peaks.T[:heads] + jnp.log(jnp.concatenate(sums, axis=0))
    lse_ref[...] = lse
    hi = lse.astype(BF16)
    rest = lse - hi.astype(F32)
    mid = rest.astype(BF16)
    low = (rest - mid.astype(F32)).astype(BF16)
    send_ref[:hd, :] = att_ref[...].astype(BF16)
    send_ref[hd : hd + heads, :] = hi
    send_ref[hd + heads : hd + 2 * heads, :] = mid
    send_ref[hd + 2 * heads :, :] = low


def merge_kernel(recv_ref, att_ref, lse_ref, gate_ref, gated_ref):
    hd = D // 2
    heads = HEADS // 2
    parts = recv_ref[hd:, :].astype(F32)
    other = parts[:heads] + parts[heads : 2 * heads] + parts[2 * heads :]
    own = lse_ref[...]
    top = jnp.maximum(own, other)
    w_own = jnp.exp(own - top)
    w_oth = jnp.exp(other - top)
    inv = 1.0 / (w_own + w_oth)
    w_own = w_own * inv
    w_oth = w_oth * inv
    pieces = []
    for h in range(heads):
        rows = slice(h * HEAD_DIM, (h + 1) * HEAD_DIM)
        att = w_own[h : h + 1] * att_ref[rows, :] + w_oth[h : h + 1] * recv_ref[rows, :].astype(F32)
        pieces.append(gate_ref[rows, :] * att)
    gated_ref[...] = jnp.concatenate(pieces, axis=0).astype(BF16)


def project_kernel(own_ref, oth_ref, wo_own_ref, wo_oth_ref, res_ref, out_ref):
    out_ref[...] = (
        res_ref[...]
        + jnp.dot(wo_own_ref[...], own_ref[...], preferred_element_type=F32)
        + jnp.dot(wo_oth_ref[...], oth_ref[...], preferred_element_type=F32)
    )


def call(kernel, outs, args, scratch=(), flops=0, trans=0, fetch=False):
    vmem = pl.BlockSpec(memory_space=pltpu.VMEM)
    source = pl.BlockSpec(memory_space=pltpu.HBM) if fetch else vmem
    if fetch:
        args = [pltpu.with_memory_space_constraint(a, pltpu.HBM) for a in args]
    nbytes = sum(math.prod(a.shape) * a.dtype.itemsize for a in (*args, *outs))
    return pl.pallas_call(
        kernel,
        out_shape=tuple(outs),
        in_specs=[source] * len(args),
        out_specs=tuple([vmem] * len(outs)),
        scratch_shapes=list(scratch),
        cost_estimate=pl.CostEstimate(flops=flops, bytes_accessed=nbytes, transcendentals=trans),
        compiler_params=pltpu.CompilerParams(vmem_limit_bytes=16 << 20),
    )(*args)


def paired_plan(
    single, pair_bias, token_mask, norm_gain, w_query, query_bias, w_key, w_value, w_gate, w_out
):
    n = single.shape[0]
    heads, _, _ = pair_bias.shape
    width = w_out.shape[1]
    hd = D // 2
    half_heads = heads // 2
    shape = jax.ShapeDtypeStruct
    swap_row = [(r * 4 + c, (1 - r) * 4 + (c ^ 1)) for r in range(2) for c in range(4)]
    swap_core = [(c, c ^ 1) for c in range(4)]
    swap_chip = [(c, c ^ 3) for c in range(4)]

    dma = pltpu.SemaphoreType.DMA(())
    (picked,) = call(pick_kernel, [shape((n // 2, D), BF16)], (single,), [dma], fetch=True)
    rows_in = lax.ppermute(picked, ("row", "col"), swap_row)
    bias_in = lax.ppermute(pair_bias, "col", swap_core)
    fetched = (
        single, norm_gain, token_mask.reshape(1, -1), w_query, query_bias, w_key, w_value, w_gate, w_out.T,
    )
    rows_other = lax.ppermute(rows_in, "col", swap_core)
    query, gate, wkv, wo_own, wo_oth, res, gain, bar = call(
        prepare_kernel,
        [
            shape((half_heads, n, hd + PAD), BF16),
            shape((hd, n), F32),
            shape((D, D), BF16),
            shape((width, hd), BF16),
            shape((width, hd), BF16),
            shape((width, n), F32),
            shape((D,), F32),
            shape((PAD, n), BF16),
        ],
        fetched,
        [
            *(pltpu.VMEM(a.shape, a.dtype) for a in fetched),
            pltpu.VMEM((D, D), F32),
            pltpu.SemaphoreType.DMA((len(fetched),)),
        ],
        flops=4 * n * D * D,
        fetch=True,
    )
    send, att, lse = call(
        partial_kernel,
        [
            shape((hd + 3 * half_heads, n), BF16),
            shape((hd, n), F32),
            shape((half_heads, n), F32),
        ],
        (rows_in, rows_other, single, gain, wkv, query, pair_bias, bias_in, bar),
        flops=4 * n * D * D,
        trans=half_heads * n * n,
    )
    recv = lax.ppermute(send, "col", swap_chip)
    (gated_own,) = call(merge_kernel, [shape((hd, n), BF16)], (recv, att, lse, gate), flops=n * D)
    gated_oth = lax.ppermute(gated_own, "col", swap_core)
    (out,) = call(
        project_kernel,
        [shape((width, n), F32)],
        (gated_own, gated_oth, wo_own, wo_oth, res),
        flops=2 * n * D * width,
    )
    return out.T


def on_device(single, pair_bias, *rest):
    heads, rows, cols = pair_bias.shape
    paired = (
        lax.axis_size("row") == 2
        and lax.axis_size("col") == 4
        and heads == HEADS
        and rows == single.shape[0]
        and 2 * cols == rows
        and cols % 128 == 0
    )
    plan = paired_plan if paired else general_plan
    return plan(single, pair_bias, *rest)


def solution(mesh):
    return jax.shard_map(
        on_device,
        mesh=mesh,
        in_specs=(
            P(("sample", "row"), None),
            P("sample", "row", "col"),
            P("sample"),
            P(),
            P(),
            P(),
            P(),
            P(),
            P(),
            P(None, "col"),
        ),
        out_specs=P(("sample", "row"), "col"),
        check_vma=False,
    )
```

```python
import math

import jax
import jax.numpy as jnp
from jax import lax
from jax.experimental import pallas as pl
from jax.experimental.pallas import tpu as pltpu
from jax.sharding import PartitionSpec as P

D = 384
HEADS = 16
EPS = 1e-05
HEAD_DIM = D // HEADS
SCALE = 1.0 / math.sqrt(HEAD_DIM)
NT = (((1,), (1,)), ((), ()))
F32 = jnp.float32
BF16 = jnp.bfloat16
PAD = 16
AHEAD = 8
CHUNK = 256
BAR_HI = -999424.0
BAR_LO = -576.0


def layer_norm(single, norm_gain):
    values_f32 = single.astype(jnp.float32)
    row_mean = jnp.mean(values_f32, axis=1, keepdims=True)
    centered = values_f32 - row_mean
    row_var = jnp.mean(centered * centered, axis=1, keepdims=True)
    return (centered * lax.rsqrt(row_var + EPS) * norm_gain).astype(jnp.bfloat16)


def attend(query_rows, key_rows, value_rows, bias_block, mask_cols):
    row_count = query_rows.shape[0]
    col_count = key_rows.shape[0]
    query_heads = query_rows.reshape(row_count, HEADS, -1)
    key_heads = key_rows.reshape(col_count, HEADS, -1)
    value_heads = value_rows.reshape(col_count, HEADS, -1)
    logits = jnp.einsum("qhd,khd->hqk", query_heads, key_heads, preferred_element_type=jnp.float32)
    mask_term = (mask_cols.astype(jnp.float32) - 1.0) * 1000000.0
    logits = logits + bias_block.astype(jnp.float32) + mask_term[None, None, :]
    row_peak = jnp.max(logits, axis=2)
    exp_scores = jnp.exp(logits - row_peak[:, :, None])
    row_total = jnp.sum(exp_scores, axis=2)
    weighted = jnp.einsum(
        "hqk,khd->qhd",
        exp_scores.astype(jnp.bfloat16),
        value_heads,
        preferred_element_type=jnp.float32,
    )
    return (row_total.T, weighted.reshape(row_count, -1))


def general_plan(
    single, pair_bias, token_mask, norm_gain, w_query, query_bias, w_key, w_value, w_gate, w_out
):
    tok_rows = single.shape[0]
    col_total = lax.axis_size("col")
    out_width = w_out.shape[1]
    col_pos = lax.axis_index("col")
    normed = layer_norm(single, norm_gain)
    query = (
        (jnp.dot(normed, w_query, preferred_element_type=jnp.float32) + query_bias) * SCALE
    ).astype(jnp.bfloat16)
    gate_act = jax.nn.sigmoid(jnp.dot(normed, w_gate, preferred_element_type=jnp.float32))
    single_cols = lax.dynamic_slice_in_dim(single, col_pos * out_width, out_width, 1).astype(
        jnp.float32
    )
    key_local = jnp.dot(normed, w_key, preferred_element_type=jnp.float32).astype(jnp.bfloat16)
    value_local = jnp.dot(normed, w_value, preferred_element_type=jnp.float32).astype(jnp.bfloat16)
    key_rows = lax.all_gather(key_local, "row", axis=0, tiled=True)
    value_rows = lax.all_gather(value_local, "row", axis=0, tiled=True)
    sub_rows = tok_rows // col_total
    query_start = col_pos * sub_rows
    bias_panel = lax.all_to_all(pair_bias, "col", split_axis=1, concat_axis=2, tiled=True)
    query_part = lax.dynamic_slice_in_dim(query, query_start, sub_rows, 0)
    gate_part = lax.dynamic_slice_in_dim(gate_act, query_start, sub_rows, 0)
    row_total, weighted = attend(query_part, key_rows, value_rows, bias_panel, token_mask)
    attended = weighted / jnp.repeat(row_total, HEAD_DIM, axis=1)
    gated_part = (gate_part * attended).astype(jnp.bfloat16)
    gated_all = lax.all_gather(gated_part, "col", axis=0, tiled=True)
    return single_cols + jnp.dot(gated_all, w_out, preferred_element_type=jnp.float32)


def place():
    col = lax.axis_index("col")
    row = lax.axis_index("row")
    chip = col // 2
    core = col % 2
    half = (chip + core) % 2
    return row, col, chip, core, half


def prepare_kernel(
    single_hbm, gain_hbm, mask_hbm, wq_hbm, bq_hbm, wk_hbm, wv_hbm, wg_hbm, wo_hbm,
    q_ref, gate_ref, wkv_ref, wo_own_ref, wo_oth_ref, res_ref, gain_out_ref, bar_ref,
    single_ref, gain_ref, mask_ref, wq_ref, bq_ref, wk_ref, wv_ref, wg_ref, wo_ref, tmp_ref, sems,
):
    _, col, chip, core, half = place()
    sources = (single_hbm, gain_hbm, wq_hbm, bq_hbm, wg_hbm, wk_hbm, wv_hbm, wo_hbm, mask_hbm)
    targets = (single_ref, gain_ref, wq_ref, bq_ref, wg_ref, wk_ref, wv_ref, wo_ref, mask_ref)
    copies = [
        pltpu.make_async_copy(src, dst, sems.at[i])
        for i, (src, dst) in enumerate(zip(sources, targets))
    ]
    for copy in copies:
        copy.start()
    hd = D // 2
    width = wo_ref.shape[0]
    n = single_ref.shape[0]
    blk = n // 2
    copies[0].wait()
    copies[1].wait()
    gain_out_ref[...] = gain_ref[...]
    x = single_ref[...].astype(F32)
    tmp_ref[:, :n] = x.T
    res_ref[...] = tmp_ref[pl.ds(pl.multiple_of(col * width, 8), width), :n]
    normed = layer_norm(single_ref[...], gain_ref[...][None, :])
    copies[2].wait()
    copies[3].wait()
    query = (jnp.dot(normed, wq_ref[...], preferred_element_type=F32) + bq_ref[...][None, :]) * SCALE
    query = jnp.where(half == 0, query[:, :hd], query[:, hd:])
    query = jnp.concatenate([query, jnp.ones((n, PAD), F32)], axis=1)
    feature = lax.broadcasted_iota(jnp.int32, query.shape, 1)
    bar_rows = (feature == hd) | (feature == hd + 1)
    for h in range(q_ref.shape[0]):
        lo = h * HEAD_DIM
        kept = ((feature >= lo) & (feature < lo + HEAD_DIM)) | bar_rows
        q_ref[h] = jnp.where(kept, query, 0.0).astype(BF16)
    copies[4].wait()
    gate = jnp.dot(normed, wg_ref[...], preferred_element_type=F32)
    tmp_ref[:, :n] = gate.T
    gate_ref[...] = jax.nn.sigmoid(tmp_ref[pl.ds(pl.multiple_of(half * hd, 8), hd), :n])
    copies[5].wait()
    tmp_ref[...] = wk_ref[...].astype(F32).T
    wkv_ref[:hd, :] = tmp_ref[pl.ds(pl.multiple_of(half * hd, 8), hd), :].astype(BF16)
    copies[6].wait()
    tmp_ref[...] = wv_ref[...].astype(F32).T
    wkv_ref[hd:, :] = tmp_ref[pl.ds(pl.multiple_of(half * hd, 8), hd), :].astype(BF16)
    copies[7].wait()
    wo = wo_ref[...].astype(F32)
    wo_own_ref[...] = jnp.where(half == 0, wo[:, :hd], wo[:, hd:]).astype(BF16)
    wo_oth_ref[...] = jnp.where(half == 0, wo[:, hd:], wo[:, :hd]).astype(BF16)
    copies[8].wait()
    base = chip * n
    first = pl.multiple_of(base + core * blk, blk)
    second = pl.multiple_of(base + (1 - core) * blk, blk)
    masked = jnp.concatenate([mask_ref[:, pl.ds(first, blk)], mask_ref[:, pl.ds(second, blk)]], axis=1)
    masked = 1.0 - masked.astype(F32)
    pad_row = lax.broadcasted_iota(jnp.int32, (PAD, n), 0)
    level = jnp.where(pad_row == 0, BAR_HI, jnp.where(pad_row == 1, BAR_LO, 0.0))
    bar_ref[...] = (level * masked).astype(BF16)


def widen_kernel(own_ref, other_ref, out_ref):
    _, _, _, _, half = place()
    heads, _, n_k = out_ref.shape
    for h in range(heads):
        out_ref[h, :, : n_k // 2] = own_ref[half * heads + h].astype(F32)
        out_ref[h, :, n_k // 2 :] = other_ref[half * heads + h].astype(F32)


def partial_kernel(
    recv_ref, own_ref, gain_ref, wkv_ref, q_ref, bias_ref, bar_ref,
    send_ref, att_ref, lse_ref,
):
    row, _, chip, core, _ = place()
    hd = D // 2
    heads = HEADS // 2
    n_q = q_ref.shape[1]
    n_k = recv_ref.shape[0]
    blk = n_k // 2
    first = pl.multiple_of(core * blk, blk)
    second = pl.multiple_of((1 - core) * blk, blk)

    local = chip == row
    block_a = jnp.where(local, own_ref[pl.ds(first, blk), :], recv_ref[pl.ds(first, blk), :])
    block_b = jnp.where(local, own_ref[pl.ds(second, blk), :], recv_ref[pl.ds(second, blk), :])
    gain = gain_ref[...][None, :]
    tokens = jnp.concatenate([block_a, block_b], axis=0)
    normed = layer_norm(tokens, gain)
    k_t = lax.dot_general(wkv_ref[:hd, :], normed, NT, preferred_element_type=F32)
    v_t = lax.dot_general(wkv_ref[hd:, :], normed, NT, preferred_element_type=F32)
    key_t = jnp.concatenate([k_t.astype(BF16), bar_ref[...]], axis=0)
    lane = lax.broadcasted_iota(jnp.int32, (n_q, 128), 1)
    peaks = jnp.zeros((n_q, 128), F32)
    ones = jnp.ones((8, n_k), F32)
    sums = []

    def logits_of(task):
        h, start = task
        return jnp.dot(q_ref[h, start : start + CHUNK, :], key_t, preferred_element_type=F32)

    tasks = [(h, start) for h in range(heads) for start in range(0, n_q, CHUNK)]
    ready = [logits_of(task) for task in tasks[:AHEAD]]
    probs, tops = [], []
    for i, (h, start) in enumerate(tasks):
        lo = h * HEAD_DIM
        rows = slice(start, start + CHUNK)
        logits = ready.pop(0)
        if i + AHEAD < len(tasks):
            ready.append(logits_of(tasks[i + AHEAD]))
        la = logits[:, :blk] + bias_ref[h, rows, :blk]
        lb = logits[:, blk:] + bias_ref[h, rows, blk:]
        peak = jnp.max(jnp.maximum(la, lb), axis=1, keepdims=True)
        probs.append(jnp.concatenate([jnp.exp(la - peak), jnp.exp(lb - peak)], axis=1).astype(BF16))
        tops.append(peak)
        if start + CHUNK < n_q:
            continue
        value = jnp.concatenate([v_t[lo : lo + HEAD_DIM], ones], axis=0).astype(BF16)
        out = lax.dot_general(
            value, jnp.concatenate(probs, axis=0), NT, preferred_element_type=F32
        )
        total = out[HEAD_DIM : HEAD_DIM + 1]
        att = out[:HEAD_DIM] / total
        att_ref[lo : lo + HEAD_DIM, :] = att
        send_ref[lo : lo + HEAD_DIM, :] = att.astype(BF16)
        sums.append(total)
        peaks = jnp.where(lane == h, jnp.concatenate(tops, axis=0), peaks)
        probs, tops = [], []
    lse = peaks.T[:heads] + jnp.log(jnp.concatenate(sums, axis=0))
    lse_ref[...] = lse
    hi = lse.astype(BF16)
    rest = lse - hi.astype(F32)
    mid = rest.astype(BF16)
    low = (rest - mid.astype(F32)).astype(BF16)
    send_ref[hd : hd + heads, :] = hi
    send_ref[hd + heads : hd + 2 * heads, :] = mid
    send_ref[hd + 2 * heads :, :] = low


def merge_kernel(recv_ref, att_ref, lse_ref, gate_ref, gated_ref):
    hd = D // 2
    heads = HEADS // 2
    parts = recv_ref[hd:, :].astype(F32)
    other = parts[:heads] + parts[heads : 2 * heads] + parts[2 * heads :]
    own = lse_ref[...]
    top = jnp.maximum(own, other)
    w_own = jnp.exp(own - top)
    w_oth = jnp.exp(other - top)
    inv = 1.0 / (w_own + w_oth)
    w_own = w_own * inv
    w_oth = w_oth * inv
    pieces = []
    for h in range(heads):
        rows = slice(h * HEAD_DIM, (h + 1) * HEAD_DIM)
        att = w_own[h : h + 1] * att_ref[rows, :] + w_oth[h : h + 1] * recv_ref[rows, :].astype(F32)
        pieces.append(gate_ref[rows, :] * att)
    gated_ref[...] = jnp.concatenate(pieces, axis=0).astype(BF16)


def project_kernel(own_ref, oth_ref, wo_own_ref, wo_oth_ref, res_ref, out_ref):
    out_ref[...] = (
        res_ref[...]
        + jnp.dot(wo_own_ref[...], own_ref[...], preferred_element_type=F32)
        + jnp.dot(wo_oth_ref[...], oth_ref[...], preferred_element_type=F32)
    )


def call(kernel, outs, args, scratch=(), flops=0, trans=0, fetch=False):
    vmem = pl.BlockSpec(memory_space=pltpu.VMEM)
    source = pl.BlockSpec(memory_space=pltpu.HBM) if fetch else vmem
    if fetch:
        args = [pltpu.with_memory_space_constraint(a, pltpu.HBM) for a in args]
    nbytes = sum(math.prod(a.shape) * a.dtype.itemsize for a in (*args, *outs))
    return pl.pallas_call(
        kernel,
        out_shape=tuple(outs),
        in_specs=[source] * len(args),
        out_specs=tuple([vmem] * len(outs)),
        scratch_shapes=list(scratch),
        cost_estimate=pl.CostEstimate(flops=flops, bytes_accessed=nbytes, transcendentals=trans),
        compiler_params=pltpu.CompilerParams(vmem_limit_bytes=16 << 20),
    )(*args)


def paired_plan(
    single, pair_bias, token_mask, norm_gain, w_query, query_bias, w_key, w_value, w_gate, w_out
):
    n = single.shape[0]
    heads, _, _ = pair_bias.shape
    width = w_out.shape[1]
    hd = D // 2
    half_heads = heads // 2
    shape = jax.ShapeDtypeStruct
    swap_row = [(r * 4 + c, (1 - r) * 4 + (c ^ 1)) for r in range(2) for c in range(4)]
    swap_core = [(c, c ^ 1) for c in range(4)]
    swap_chip = [(c, c ^ 3) for c in range(4)]

    single_in = lax.ppermute(single, ("row", "col"), swap_row)
    bias_in = lax.ppermute(pair_bias, "col", swap_core)
    fetched = (
        single, norm_gain, token_mask.reshape(1, -1), w_query, query_bias, w_key, w_value, w_gate, w_out.T,
    )
    query, gate, wkv, wo_own, wo_oth, res, gain, bar = call(
        prepare_kernel,
        [
            shape((half_heads, n, hd + PAD), BF16),
            shape((hd, n), F32),
            shape((D, D), BF16),
            shape((width, hd), BF16),
            shape((width, hd), BF16),
            shape((width, n), F32),
            shape((D,), F32),
            shape((PAD, n), BF16),
        ],
        fetched,
        [
            *(pltpu.VMEM(a.shape, a.dtype) for a in fetched),
            pltpu.VMEM((D, D), F32),
            pltpu.SemaphoreType.DMA((len(fetched),)),
        ],
        flops=4 * n * D * D,
        fetch=True,
    )
    (bias,) = call(
        widen_kernel, [shape((half_heads, n, n), F32)], (pair_bias, bias_in), flops=half_heads * n * n
    )
    send, att, lse = call(
        partial_kernel,
        [
            shape((hd + 3 * half_heads, n), BF16),
            shape((hd, n), F32),
            shape((half_heads, n), F32),
        ],
        (single_in, single, gain, wkv, query, bias, bar),
        flops=4 * n * D * D,
        trans=half_heads * n * n,
    )
    recv = lax.ppermute(send, "col", swap_chip)
    (gated_own,) = call(merge_kernel, [shape((hd, n), BF16)], (recv, att, lse, gate), flops=n * D)
    gated_oth = lax.ppermute(gated_own, "col", swap_core)
    (out,) = call(
        project_kernel,
        [shape((width, n), F32)],
        (gated_own, gated_oth, wo_own, wo_oth, res),
        flops=2 * n * D * width,
    )
    return out.T


def on_device(single, pair_bias, *rest):
    heads, rows, cols = pair_bias.shape
    paired = (
        lax.axis_size("row") == 2
        and lax.axis_size("col") == 4
        and heads == HEADS
        and rows == single.shape[0]
        and 2 * cols == rows
        and cols % 128 == 0
    )
    plan = paired_plan if paired else general_plan
    return plan(single, pair_bias, *rest)


def solution(mesh):
    return jax.shard_map(
        on_device,
        mesh=mesh,
        in_specs=(
            P(("sample", "row"), None),
            P("sample", "row", "col"),
            P("sample"),
            P(),
            P(),
            P(),
            P(),
            P(),
            P(),
            P(None, "col"),
        ),
        out_specs=P(("sample", "row"), "col"),
        check_vma=False,
    )
```

```python
import math

import jax
import jax.numpy as jnp
from jax import lax
from jax.experimental import pallas as pl
from jax.experimental.pallas import tpu as pltpu
from jax.sharding import PartitionSpec as P

D = 384
HEADS = 16
EPS = 1e-05
HEAD_DIM = D // HEADS
SCALE = 1.0 / math.sqrt(HEAD_DIM)
NT = (((1,), (1,)), ((), ()))
F32 = jnp.float32
BF16 = jnp.bfloat16
PAD = 16
AHEAD = 8
CHUNK = 256
BAR_HI = -999424.0
BAR_LO = -576.0


def layer_norm(single, norm_gain):
    values_f32 = single.astype(jnp.float32)
    row_mean = jnp.mean(values_f32, axis=1, keepdims=True)
    centered = values_f32 - row_mean
    row_var = jnp.mean(centered * centered, axis=1, keepdims=True)
    return (centered * lax.rsqrt(row_var + EPS) * norm_gain).astype(jnp.bfloat16)


def attend(query_rows, key_rows, value_rows, bias_block, mask_cols):
    row_count = query_rows.shape[0]
    col_count = key_rows.shape[0]
    query_heads = query_rows.reshape(row_count, HEADS, -1)
    key_heads = key_rows.reshape(col_count, HEADS, -1)
    value_heads = value_rows.reshape(col_count, HEADS, -1)
    logits = jnp.einsum("qhd,khd->hqk", query_heads, key_heads, preferred_element_type=jnp.float32)
    mask_term = (mask_cols.astype(jnp.float32) - 1.0) * 1000000.0
    logits = logits + bias_block.astype(jnp.float32) + mask_term[None, None, :]
    row_peak = jnp.max(logits, axis=2)
    exp_scores = jnp.exp(logits - row_peak[:, :, None])
    row_total = jnp.sum(exp_scores, axis=2)
    weighted = jnp.einsum(
        "hqk,khd->qhd",
        exp_scores.astype(jnp.bfloat16),
        value_heads,
        preferred_element_type=jnp.float32,
    )
    return (row_total.T, weighted.reshape(row_count, -1))


def general_plan(
    single, pair_bias, token_mask, norm_gain, w_query, query_bias, w_key, w_value, w_gate, w_out
):
    tok_rows = single.shape[0]
    col_total = lax.axis_size("col")
    out_width = w_out.shape[1]
    col_pos = lax.axis_index("col")
    normed = layer_norm(single, norm_gain)
    query = (
        (jnp.dot(normed, w_query, preferred_element_type=jnp.float32) + query_bias) * SCALE
    ).astype(jnp.bfloat16)
    gate_act = jax.nn.sigmoid(jnp.dot(normed, w_gate, preferred_element_type=jnp.float32))
    single_cols = lax.dynamic_slice_in_dim(single, col_pos * out_width, out_width, 1).astype(
        jnp.float32
    )
    key_local = jnp.dot(normed, w_key, preferred_element_type=jnp.float32).astype(jnp.bfloat16)
    value_local = jnp.dot(normed, w_value, preferred_element_type=jnp.float32).astype(jnp.bfloat16)
    key_rows = lax.all_gather(key_local, "row", axis=0, tiled=True)
    value_rows = lax.all_gather(value_local, "row", axis=0, tiled=True)
    sub_rows = tok_rows // col_total
    query_start = col_pos * sub_rows
    bias_panel = lax.all_to_all(pair_bias, "col", split_axis=1, concat_axis=2, tiled=True)
    query_part = lax.dynamic_slice_in_dim(query, query_start, sub_rows, 0)
    gate_part = lax.dynamic_slice_in_dim(gate_act, query_start, sub_rows, 0)
    row_total, weighted = attend(query_part, key_rows, value_rows, bias_panel, token_mask)
    attended = weighted / jnp.repeat(row_total, HEAD_DIM, axis=1)
    gated_part = (gate_part * attended).astype(jnp.bfloat16)
    gated_all = lax.all_gather(gated_part, "col", axis=0, tiled=True)
    return single_cols + jnp.dot(gated_all, w_out, preferred_element_type=jnp.float32)


def place():
    col = lax.axis_index("col")
    row = lax.axis_index("row")
    chip = col // 2
    core = col % 2
    half = (chip + core) % 2
    return row, col, chip, core, half


def prepare_kernel(
    single_hbm, gain_hbm, mask_hbm, wq_hbm, bq_hbm, wk_hbm, wv_hbm, wg_hbm, wo_hbm,
    q_ref, gate_ref, wkv_ref, wo_own_ref, wo_oth_ref, res_ref, gain_out_ref, bar_ref,
    single_ref, gain_ref, mask_ref, wq_ref, bq_ref, wk_ref, wv_ref, wg_ref, wo_ref, tmp_ref, sems,
):
    _, col, chip, core, half = place()
    sources = (single_hbm, gain_hbm, wq_hbm, bq_hbm, wg_hbm, wk_hbm, wv_hbm, wo_hbm, mask_hbm)
    targets = (single_ref, gain_ref, wq_ref, bq_ref, wg_ref, wk_ref, wv_ref, wo_ref, mask_ref)
    copies = [
        pltpu.make_async_copy(src, dst, sems.at[i])
        for i, (src, dst) in enumerate(zip(sources, targets))
    ]
    for copy in copies:
        copy.start()
    hd = D // 2
    width = wo_ref.shape[0]
    n = single_ref.shape[0]
    blk = n // 2
    copies[0].wait()
    copies[1].wait()
    gain_out_ref[...] = gain_ref[...]
    x = single_ref[...].astype(F32)
    tmp_ref[:, :n] = x.T
    res_ref[...] = tmp_ref[pl.ds(pl.multiple_of(col * width, 8), width), :n]
    normed = layer_norm(single_ref[...], gain_ref[...][None, :])
    copies[2].wait()
    copies[3].wait()
    query = (jnp.dot(normed, wq_ref[...], preferred_element_type=F32) + bq_ref[...][None, :]) * SCALE
    query = jnp.where(half == 0, query[:, :hd], query[:, hd:])
    query = jnp.concatenate([query, jnp.ones((n, PAD), F32)], axis=1)
    feature = lax.broadcasted_iota(jnp.int32, query.shape, 1)
    bar_rows = (feature == hd) | (feature == hd + 1)
    for h in range(q_ref.shape[0]):
        lo = h * HEAD_DIM
        kept = ((feature >= lo) & (feature < lo + HEAD_DIM)) | bar_rows
        q_ref[h] = jnp.where(kept, query, 0.0).astype(BF16)
    copies[4].wait()
    gate = jnp.dot(normed, wg_ref[...], preferred_element_type=F32)
    tmp_ref[:, :n] = gate.T
    gate_ref[...] = jax.nn.sigmoid(tmp_ref[pl.ds(pl.multiple_of(half * hd, 8), hd), :n])
    copies[5].wait()
    tmp_ref[...] = wk_ref[...].astype(F32).T
    wkv_ref[:hd, :] = tmp_ref[pl.ds(pl.multiple_of(half * hd, 8), hd), :].astype(BF16)
    copies[6].wait()
    tmp_ref[...] = wv_ref[...].astype(F32).T
    wkv_ref[hd:, :] = tmp_ref[pl.ds(pl.multiple_of(half * hd, 8), hd), :].astype(BF16)
    copies[7].wait()
    wo = wo_ref[...].astype(F32)
    wo_own_ref[...] = jnp.where(half == 0, wo[:, :hd], wo[:, hd:]).astype(BF16)
    wo_oth_ref[...] = jnp.where(half == 0, wo[:, hd:], wo[:, :hd]).astype(BF16)
    copies[8].wait()
    base = chip * n
    first = pl.multiple_of(base + core * blk, blk)
    second = pl.multiple_of(base + (1 - core) * blk, blk)
    masked = jnp.concatenate([mask_ref[:, pl.ds(first, blk)], mask_ref[:, pl.ds(second, blk)]], axis=1)
    masked = 1.0 - masked.astype(F32)
    pad_row = lax.broadcasted_iota(jnp.int32, (PAD, n), 0)
    level = jnp.where(pad_row == 0, BAR_HI, jnp.where(pad_row == 1, BAR_LO, 0.0))
    bar_ref[...] = (level * masked).astype(BF16)


def widen_kernel(own_ref, other_ref, out_ref):
    _, _, _, _, half = place()
    heads, _, n_k = out_ref.shape
    for h in range(heads):
        out_ref[h, :, : n_k // 2] = own_ref[half * heads + h].astype(F32)
        out_ref[h, :, n_k // 2 :] = other_ref[half * heads + h].astype(F32)


def partial_kernel(
    recv_ref, own_ref, gain_ref, wkv_ref, q_ref, bias_ref, bar_ref,
    send_ref, att_ref, lse_ref,
):
    row, _, chip, core, _ = place()
    hd = D // 2
    heads = HEADS // 2
    n_q = q_ref.shape[1]
    n_k = recv_ref.shape[0]
    blk = n_k // 2
    first = pl.multiple_of(core * blk, blk)
    second = pl.multiple_of((1 - core) * blk, blk)

    local = chip == row
    block_a = jnp.where(local, own_ref[pl.ds(first, blk), :], recv_ref[pl.ds(first, blk), :])
    block_b = jnp.where(local, own_ref[pl.ds(second, blk), :], recv_ref[pl.ds(second, blk), :])
    gain = gain_ref[...][None, :]
    parts = [layer_norm(block, gain) for block in (block_a, block_b)]
    normed = jnp.concatenate(parts, axis=0)
    k_t = lax.dot_general(wkv_ref[:hd, :], normed, NT, preferred_element_type=F32)
    v_t = lax.dot_general(wkv_ref[hd:, :], normed, NT, preferred_element_type=F32)
    key_t = jnp.concatenate([k_t.astype(BF16), bar_ref[...]], axis=0)
    lane = lax.broadcasted_iota(jnp.int32, (n_q, 128), 1)
    peaks = jnp.zeros((n_q, 128), F32)
    ones = jnp.ones((8, n_k), F32)
    sums = []

    def logits_of(task):
        h, start = task
        return jnp.dot(q_ref[h, start : start + CHUNK, :], key_t, preferred_element_type=F32)

    tasks = [(h, start) for h in range(heads) for start in range(0, n_q, CHUNK)]
    ready = [logits_of(task) for task in tasks[:AHEAD]]
    probs, tops = [], []
    for i, (h, start) in enumerate(tasks):
        lo = h * HEAD_DIM
        rows = slice(start, start + CHUNK)
        logits = ready.pop(0)
        if i + AHEAD < len(tasks):
            ready.append(logits_of(tasks[i + AHEAD]))
        la = logits[:, :blk] + bias_ref[h, rows, :blk]
        lb = logits[:, blk:] + bias_ref[h, rows, blk:]
        peak = jnp.max(jnp.maximum(la, lb), axis=1, keepdims=True)
        probs.append(jnp.concatenate([jnp.exp(la - peak), jnp.exp(lb - peak)], axis=1).astype(BF16))
        tops.append(peak)
        if start + CHUNK < n_q:
            continue
        value = jnp.concatenate([v_t[lo : lo + HEAD_DIM], ones], axis=0).astype(BF16)
        out = lax.dot_general(
            value, jnp.concatenate(probs, axis=0), NT, preferred_element_type=F32
        )
        total = out[HEAD_DIM : HEAD_DIM + 1]
        att = out[:HEAD_DIM] / total
        att_ref[lo : lo + HEAD_DIM, :] = att
        send_ref[lo : lo + HEAD_DIM, :] = att.astype(BF16)
        sums.append(total)
        peaks = jnp.where(lane == h, jnp.concatenate(tops, axis=0), peaks)
        probs, tops = [], []
    lse = peaks.T[:heads] + jnp.log(jnp.concatenate(sums, axis=0))
    lse_ref[...] = lse
    hi = lse.astype(BF16)
    rest = lse - hi.astype(F32)
    mid = rest.astype(BF16)
    low = (rest - mid.astype(F32)).astype(BF16)
    send_ref[hd : hd + heads, :] = hi
    send_ref[hd + heads : hd + 2 * heads, :] = mid
    send_ref[hd + 2 * heads :, :] = low


def merge_kernel(recv_ref, att_ref, lse_ref, gate_ref, gated_ref):
    hd = D // 2
    heads = HEADS // 2
    parts = recv_ref[hd:, :].astype(F32)
    other = parts[:heads] + parts[heads : 2 * heads] + parts[2 * heads :]
    own = lse_ref[...]
    top = jnp.maximum(own, other)
    w_own = jnp.exp(own - top)
    w_oth = jnp.exp(other - top)
    inv = 1.0 / (w_own + w_oth)
    w_own = w_own * inv
    w_oth = w_oth * inv
    pieces = []
    for h in range(heads):
        rows = slice(h * HEAD_DIM, (h + 1) * HEAD_DIM)
        att = w_own[h : h + 1] * att_ref[rows, :] + w_oth[h : h + 1] * recv_ref[rows, :].astype(F32)
        pieces.append(gate_ref[rows, :] * att)
    gated_ref[...] = jnp.concatenate(pieces, axis=0).astype(BF16)


def project_kernel(own_ref, oth_ref, wo_own_ref, wo_oth_ref, res_ref, out_ref):
    out_ref[...] = (
        res_ref[...]
        + jnp.dot(wo_own_ref[...], own_ref[...], preferred_element_type=F32)
        + jnp.dot(wo_oth_ref[...], oth_ref[...], preferred_element_type=F32)
    )


def call(kernel, outs, args, scratch=(), flops=0, trans=0, fetch=False):
    vmem = pl.BlockSpec(memory_space=pltpu.VMEM)
    source = pl.BlockSpec(memory_space=pltpu.HBM) if fetch else vmem
    if fetch:
        args = [pltpu.with_memory_space_constraint(a, pltpu.HBM) for a in args]
    nbytes = sum(math.prod(a.shape) * a.dtype.itemsize for a in (*args, *outs))
    return pl.pallas_call(
        kernel,
        out_shape=tuple(outs),
        in_specs=[source] * len(args),
        out_specs=tuple([vmem] * len(outs)),
        scratch_shapes=list(scratch),
        cost_estimate=pl.CostEstimate(flops=flops, bytes_accessed=nbytes, transcendentals=trans),
        compiler_params=pltpu.CompilerParams(vmem_limit_bytes=16 << 20),
    )(*args)


def paired_plan(
    single, pair_bias, token_mask, norm_gain, w_query, query_bias, w_key, w_value, w_gate, w_out
):
    n = single.shape[0]
    heads, _, _ = pair_bias.shape
    width = w_out.shape[1]
    hd = D // 2
    half_heads = heads // 2
    shape = jax.ShapeDtypeStruct
    swap_row = [(r * 4 + c, (1 - r) * 4 + (c ^ 1)) for r in range(2) for c in range(4)]
    swap_core = [(c, c ^ 1) for c in range(4)]
    swap_chip = [(c, c ^ 3) for c in range(4)]

    single_in = lax.ppermute(single, ("row", "col"), swap_row)
    bias_in = lax.ppermute(pair_bias, "col", swap_core)
    fetched = (
        single, norm_gain, token_mask.reshape(1, -1), w_query, query_bias, w_key, w_value, w_gate, w_out.T,
    )
    query, gate, wkv, wo_own, wo_oth, res, gain, bar = call(
        prepare_kernel,
        [
            shape((half_heads, n, hd + PAD), BF16),
            shape((hd, n), F32),
            shape((D, D), BF16),
            shape((width, hd), BF16),
            shape((width, hd), BF16),
            shape((width, n), F32),
            shape((D,), F32),
            shape((PAD, n), BF16),
        ],
        fetched,
        [
            *(pltpu.VMEM(a.shape, a.dtype) for a in fetched),
            pltpu.VMEM((D, D), F32),
            pltpu.SemaphoreType.DMA((len(fetched),)),
        ],
        flops=4 * n * D * D,
        fetch=True,
    )
    (bias,) = call(
        widen_kernel, [shape((half_heads, n, n), F32)], (pair_bias, bias_in), flops=half_heads * n * n
    )
    send, att, lse = call(
        partial_kernel,
        [
            shape((hd + 3 * half_heads, n), BF16),
            shape((hd, n), F32),
            shape((half_heads, n), F32),
        ],
        (single_in, single, gain, wkv, query, bias, bar),
        flops=4 * n * D * D,
        trans=half_heads * n * n,
    )
    recv = lax.ppermute(send, "col", swap_chip)
    (gated_own,) = call(merge_kernel, [shape((hd, n), BF16)], (recv, att, lse, gate), flops=n * D)
    gated_oth = lax.ppermute(gated_own, "col", swap_core)
    (out,) = call(
        project_kernel,
        [shape((width, n), F32)],
        (gated_own, gated_oth, wo_own, wo_oth, res),
        flops=2 * n * D * width,
    )
    return out.T


def on_device(single, pair_bias, *rest):
    heads, rows, cols = pair_bias.shape
    paired = (
        lax.axis_size("row") == 2
        and lax.axis_size("col") == 4
        and heads == HEADS
        and rows == single.shape[0]
        and 2 * cols == rows
        and cols % 128 == 0
    )
    plan = paired_plan if paired else general_plan
    return plan(single, pair_bias, *rest)


def solution(mesh):
    return jax.shard_map(
        on_device,
        mesh=mesh,
        in_specs=(
            P(("sample", "row"), None),
            P("sample", "row", "col"),
            P("sample"),
            P(),
            P(),
            P(),
            P(),
            P(),
            P(),
            P(None, "col"),
        ),
        out_specs=P(("sample", "row"), "col"),
        check_vma=False,
    )
```

```python
import math

import jax
import jax.numpy as jnp
from jax import lax
from jax.experimental import pallas as pl
from jax.experimental.pallas import tpu as pltpu
from jax.sharding import PartitionSpec as P

D = 384
HEADS = 16
EPS = 1e-05
HEAD_DIM = D // HEADS
SCALE = 1.0 / math.sqrt(HEAD_DIM)
NT = (((1,), (1,)), ((), ()))
F32 = jnp.float32
BF16 = jnp.bfloat16
PAD = 16
AHEAD = 8
CHUNK = 256
BAR_HI = -999424.0
BAR_LO = -576.0


def layer_norm(single, norm_gain):
    values_f32 = single.astype(jnp.float32)
    row_mean = jnp.mean(values_f32, axis=1, keepdims=True)
    centered = values_f32 - row_mean
    row_var = jnp.mean(centered * centered, axis=1, keepdims=True)
    return (centered * lax.rsqrt(row_var + EPS) * norm_gain).astype(jnp.bfloat16)


def attend(query_rows, key_rows, value_rows, bias_block, mask_cols):
    row_count = query_rows.shape[0]
    col_count = key_rows.shape[0]
    query_heads = query_rows.reshape(row_count, HEADS, -1)
    key_heads = key_rows.reshape(col_count, HEADS, -1)
    value_heads = value_rows.reshape(col_count, HEADS, -1)
    logits = jnp.einsum("qhd,khd->hqk", query_heads, key_heads, preferred_element_type=jnp.float32)
    mask_term = (mask_cols.astype(jnp.float32) - 1.0) * 1000000.0
    logits = logits + bias_block.astype(jnp.float32) + mask_term[None, None, :]
    row_peak = jnp.max(logits, axis=2)
    exp_scores = jnp.exp(logits - row_peak[:, :, None])
    row_total = jnp.sum(exp_scores, axis=2)
    weighted = jnp.einsum(
        "hqk,khd->qhd",
        exp_scores.astype(jnp.bfloat16),
        value_heads,
        preferred_element_type=jnp.float32,
    )
    return (row_total.T, weighted.reshape(row_count, -1))


def general_plan(
    single, pair_bias, token_mask, norm_gain, w_query, query_bias, w_key, w_value, w_gate, w_out
):
    tok_rows = single.shape[0]
    col_total = lax.axis_size("col")
    out_width = w_out.shape[1]
    col_pos = lax.axis_index("col")
    normed = layer_norm(single, norm_gain)
    query = (
        (jnp.dot(normed, w_query, preferred_element_type=jnp.float32) + query_bias) * SCALE
    ).astype(jnp.bfloat16)
    gate_act = jax.nn.sigmoid(jnp.dot(normed, w_gate, preferred_element_type=jnp.float32))
    single_cols = lax.dynamic_slice_in_dim(single, col_pos * out_width, out_width, 1).astype(
        jnp.float32
    )
    key_local = jnp.dot(normed, w_key, preferred_element_type=jnp.float32).astype(jnp.bfloat16)
    value_local = jnp.dot(normed, w_value, preferred_element_type=jnp.float32).astype(jnp.bfloat16)
    key_rows = lax.all_gather(key_local, "row", axis=0, tiled=True)
    value_rows = lax.all_gather(value_local, "row", axis=0, tiled=True)
    sub_rows = tok_rows // col_total
    query_start = col_pos * sub_rows
    bias_panel = lax.all_to_all(pair_bias, "col", split_axis=1, concat_axis=2, tiled=True)
    query_part = lax.dynamic_slice_in_dim(query, query_start, sub_rows, 0)
    gate_part = lax.dynamic_slice_in_dim(gate_act, query_start, sub_rows, 0)
    row_total, weighted = attend(query_part, key_rows, value_rows, bias_panel, token_mask)
    attended = weighted / jnp.repeat(row_total, HEAD_DIM, axis=1)
    gated_part = (gate_part * attended).astype(jnp.bfloat16)
    gated_all = lax.all_gather(gated_part, "col", axis=0, tiled=True)
    return single_cols + jnp.dot(gated_all, w_out, preferred_element_type=jnp.float32)


def place():
    col = lax.axis_index("col")
    row = lax.axis_index("row")
    chip = col // 2
    core = col % 2
    half = (chip + core) % 2
    return row, col, chip, core, half


def prepare_kernel(
    single_hbm, gain_hbm, mask_hbm, wq_hbm, bq_hbm, wk_hbm, wv_hbm, wg_hbm, wo_hbm,
    q_ref, gate_ref, wkv_ref, wo_own_ref, wo_oth_ref, res_ref, gain_out_ref, bar_ref,
    single_ref, gain_ref, mask_ref, wq_ref, bq_ref, wk_ref, wv_ref, wg_ref, wo_ref, tmp_ref, sems,
):
    _, col, chip, core, half = place()
    sources = (single_hbm, gain_hbm, wq_hbm, bq_hbm, wg_hbm, wk_hbm, wv_hbm, wo_hbm, mask_hbm)
    targets = (single_ref, gain_ref, wq_ref, bq_ref, wg_ref, wk_ref, wv_ref, wo_ref, mask_ref)
    copies = [
        pltpu.make_async_copy(src, dst, sems.at[i])
        for i, (src, dst) in enumerate(zip(sources, targets))
    ]
    for copy in copies:
        copy.start()
    hd = D // 2
    width = wo_ref.shape[0]
    n = single_ref.shape[0]
    blk = n // 2
    copies[0].wait()
    copies[1].wait()
    gain_out_ref[...] = gain_ref[...]
    x = single_ref[...].astype(F32)
    tmp_ref[:, :n] = x.T
    res_ref[...] = tmp_ref[pl.ds(pl.multiple_of(col * width, 8), width), :n]
    normed = layer_norm(single_ref[...], gain_ref[...][None, :])
    copies[2].wait()
    copies[3].wait()
    query = (jnp.dot(normed, wq_ref[...], preferred_element_type=F32) + bq_ref[...][None, :]) * SCALE
    query = jnp.where(half == 0, query[:, :hd], query[:, hd:])
    query = jnp.concatenate([query, jnp.ones((n, PAD), F32)], axis=1)
    feature = lax.broadcasted_iota(jnp.int32, query.shape, 1)
    bar_rows = (feature == hd) | (feature == hd + 1)
    for h in range(q_ref.shape[0]):
        lo = h * HEAD_DIM
        kept = ((feature >= lo) & (feature < lo + HEAD_DIM)) | bar_rows
        q_ref[h] = jnp.where(kept, query, 0.0).astype(BF16)
    copies[4].wait()
    gate = jnp.dot(normed, wg_ref[...], preferred_element_type=F32)
    tmp_ref[:, :n] = gate.T
    gate_ref[...] = jax.nn.sigmoid(tmp_ref[pl.ds(pl.multiple_of(half * hd, 8), hd), :n])
    copies[5].wait()
    tmp_ref[...] = wk_ref[...].astype(F32).T
    wkv_ref[:hd, :] = tmp_ref[pl.ds(pl.multiple_of(half * hd, 8), hd), :].astype(BF16)
    copies[6].wait()
    tmp_ref[...] = wv_ref[...].astype(F32).T
    wkv_ref[hd:, :] = tmp_ref[pl.ds(pl.multiple_of(half * hd, 8), hd), :].astype(BF16)
    copies[7].wait()
    wo = wo_ref[...].astype(F32)
    wo_own_ref[...] = jnp.where(half == 0, wo[:, :hd], wo[:, hd:]).astype(BF16)
    wo_oth_ref[...] = jnp.where(half == 0, wo[:, hd:], wo[:, :hd]).astype(BF16)
    copies[8].wait()
    base = chip * n
    first = pl.multiple_of(base + core * blk, blk)
    second = pl.multiple_of(base + (1 - core) * blk, blk)
    masked = jnp.concatenate([mask_ref[:, pl.ds(first, blk)], mask_ref[:, pl.ds(second, blk)]], axis=1)
    masked = 1.0 - masked.astype(F32)
    pad_row = lax.broadcasted_iota(jnp.int32, (PAD, n), 0)
    level = jnp.where(pad_row == 0, BAR_HI, jnp.where(pad_row == 1, BAR_LO, 0.0))
    bar_ref[...] = (level * masked).astype(BF16)


def widen_kernel(own_ref, other_ref, out_ref):
    _, _, _, _, half = place()
    heads, _, n_k = out_ref.shape
    for h in range(heads):
        out_ref[h, :, : n_k // 2] = own_ref[half * heads + h].astype(F32)
        out_ref[h, :, n_k // 2 :] = other_ref[half * heads + h].astype(F32)


def partial_kernel(
    recv_ref, own_ref, gain_ref, wkv_ref, q_ref, bias_ref, bar_ref,
    send_ref, att_ref, lse_ref,
):
    row, _, chip, core, _ = place()
    hd = D // 2
    heads = HEADS // 2
    n_q = q_ref.shape[1]
    n_k = recv_ref.shape[0]
    blk = n_k // 2
    first = pl.multiple_of(core * blk, blk)
    second = pl.multiple_of((1 - core) * blk, blk)

    local = chip == row
    block_a = jnp.where(local, own_ref[pl.ds(first, blk), :], recv_ref[pl.ds(first, blk), :])
    block_b = jnp.where(local, own_ref[pl.ds(second, blk), :], recv_ref[pl.ds(second, blk), :])
    gain = gain_ref[...][None, :]
    parts = [layer_norm(block, gain) for block in (block_a, block_b)]
    normed = jnp.concatenate(parts, axis=0)
    k_t = lax.dot_general(wkv_ref[:hd, :], normed, NT, preferred_element_type=F32)
    v_t = lax.dot_general(wkv_ref[hd:, :], normed, NT, preferred_element_type=F32)
    key_t = jnp.concatenate([k_t.astype(BF16), bar_ref[...]], axis=0)
    lane = lax.broadcasted_iota(jnp.int32, (n_q, 128), 1)
    peaks = jnp.zeros((n_q, 128), F32)
    ones = jnp.ones((8, n_k), F32)
    sums = []

    def logits_of(task):
        h, start = task
        return jnp.dot(q_ref[h, start : start + CHUNK, :], key_t, preferred_element_type=F32)

    tasks = [(h, start) for h in range(heads) for start in range(0, n_q, CHUNK)]
    ready = [logits_of(task) for task in tasks[:AHEAD]]
    probs, tops = [], []
    for i, (h, start) in enumerate(tasks):
        lo = h * HEAD_DIM
        rows = slice(start, start + CHUNK)
        logits = ready.pop(0)
        if i + AHEAD < len(tasks):
            ready.append(logits_of(tasks[i + AHEAD]))
        la = logits[:, :blk] + bias_ref[h, rows, :blk]
        lb = logits[:, blk:] + bias_ref[h, rows, blk:]
        peak = jnp.max(jnp.maximum(la, lb), axis=1, keepdims=True)
        probs.append(jnp.concatenate([jnp.exp(la - peak), jnp.exp(lb - peak)], axis=1).astype(BF16))
        tops.append(peak)
        if start + CHUNK < n_q:
            continue
        value = jnp.concatenate([v_t[lo : lo + HEAD_DIM], ones], axis=0).astype(BF16)
        out = lax.dot_general(
            value, jnp.concatenate(probs, axis=0), NT, preferred_element_type=F32
        )
        total = out[HEAD_DIM : HEAD_DIM + 1]
        att = out[:HEAD_DIM] / total
        att_ref[lo : lo + HEAD_DIM, :] = att
        send_ref[lo : lo + HEAD_DIM, :] = att.astype(BF16)
        sums.append(total)
        peaks = jnp.where(lane == h, jnp.concatenate(tops, axis=0), peaks)
        probs, tops = [], []
    lse = peaks.T[:heads] + jnp.log(jnp.concatenate(sums, axis=0))
    lse_ref[...] = lse
    hi = lse.astype(BF16)
    rest = lse - hi.astype(F32)
    mid = rest.astype(BF16)
    low = (rest - mid.astype(F32)).astype(BF16)
    send_ref[hd : hd + heads, :] = hi
    send_ref[hd + heads : hd + 2 * heads, :] = mid
    send_ref[hd + 2 * heads :, :] = low


def merge_kernel(recv_ref, att_ref, lse_ref, gate_ref, gated_ref):
    hd = D // 2
    heads = HEADS // 2
    parts = recv_ref[hd:, :].astype(F32)
    other = parts[:heads] + parts[heads : 2 * heads] + parts[2 * heads :]
    own = lse_ref[...]
    top = jnp.maximum(own, other)
    w_own = jnp.exp(own - top)
    w_oth = jnp.exp(other - top)
    inv = 1.0 / (w_own + w_oth)
    w_own = w_own * inv
    w_oth = w_oth * inv
    pieces = []
    for h in range(heads):
        rows = slice(h * HEAD_DIM, (h + 1) * HEAD_DIM)
        att = w_own[h : h + 1] * att_ref[rows, :] + w_oth[h : h + 1] * recv_ref[rows, :].astype(F32)
        pieces.append(gate_ref[rows, :] * att)
    gated_ref[...] = jnp.concatenate(pieces, axis=0).astype(BF16)


def own_project_kernel(own_ref, wo_own_ref, res_ref, acc_ref):
    acc_ref[...] = res_ref[...] + jnp.dot(wo_own_ref[...], own_ref[...], preferred_element_type=F32)


def project_kernel(acc_ref, oth_ref, wo_oth_ref, out_ref):
    out_ref[...] = acc_ref[...] + jnp.dot(
        wo_oth_ref[...], oth_ref[...], preferred_element_type=F32
    )


def call(kernel, outs, args, scratch=(), flops=0, trans=0, fetch=False):
    vmem = pl.BlockSpec(memory_space=pltpu.VMEM)
    source = pl.BlockSpec(memory_space=pltpu.HBM) if fetch else vmem
    if fetch:
        args = [pltpu.with_memory_space_constraint(a, pltpu.HBM) for a in args]
    nbytes = sum(math.prod(a.shape) * a.dtype.itemsize for a in (*args, *outs))
    return pl.pallas_call(
        kernel,
        out_shape=tuple(outs),
        in_specs=[source] * len(args),
        out_specs=tuple([vmem] * len(outs)),
        scratch_shapes=list(scratch),
        cost_estimate=pl.CostEstimate(flops=flops, bytes_accessed=nbytes, transcendentals=trans),
        compiler_params=pltpu.CompilerParams(vmem_limit_bytes=16 << 20),
    )(*args)


def paired_plan(
    single, pair_bias, token_mask, norm_gain, w_query, query_bias, w_key, w_value, w_gate, w_out
):
    n = single.shape[0]
    heads, _, _ = pair_bias.shape
    width = w_out.shape[1]
    hd = D // 2
    half_heads = heads // 2
    shape = jax.ShapeDtypeStruct
    swap_row = [(r * 4 + c, (1 - r) * 4 + (c ^ 1)) for r in range(2) for c in range(4)]
    swap_core = [(c, c ^ 1) for c in range(4)]
    swap_chip = [(c, c ^ 3) for c in range(4)]

    single_in = lax.ppermute(single, ("row", "col"), swap_row)
    bias_in = lax.ppermute(pair_bias, "col", swap_core)
    fetched = (
        single, norm_gain, token_mask.reshape(1, -1), w_query, query_bias, w_key, w_value, w_gate, w_out.T,
    )
    query, gate, wkv, wo_own, wo_oth, res, gain, bar = call(
        prepare_kernel,
        [
            shape((half_heads, n, hd + PAD), BF16),
            shape((hd, n), F32),
            shape((D, D), BF16),
            shape((width, hd), BF16),
            shape((width, hd), BF16),
            shape((width, n), F32),
            shape((D,), F32),
            shape((PAD, n), BF16),
        ],
        fetched,
        [
            *(pltpu.VMEM(a.shape, a.dtype) for a in fetched),
            pltpu.VMEM((D, D), F32),
            pltpu.SemaphoreType.DMA((len(fetched),)),
        ],
        flops=4 * n * D * D,
        fetch=True,
    )
    (bias,) = call(
        widen_kernel, [shape((half_heads, n, n), F32)], (pair_bias, bias_in), flops=half_heads * n * n
    )
    send, att, lse = call(
        partial_kernel,
        [
            shape((hd + 3 * half_heads, n), BF16),
            shape((hd, n), F32),
            shape((half_heads, n), F32),
        ],
        (single_in, single, gain, wkv, query, bias, bar),
        flops=4 * n * D * D,
        trans=half_heads * n * n,
    )
    recv = lax.ppermute(send, "col", swap_chip)
    (gated_own,) = call(merge_kernel, [shape((hd, n), BF16)], (recv, att, lse, gate), flops=n * D)
    gated_oth = lax.ppermute(gated_own, "col", swap_core)
    (acc,) = call(
        own_project_kernel,
        [shape((width, n), F32)],
        (gated_own, wo_own, res),
        flops=n * D * width,
    )
    (out,) = call(
        project_kernel, [shape((width, n), F32)], (acc, gated_oth, wo_oth), flops=n * D * width
    )
    return out.T


def on_device(single, pair_bias, *rest):
    heads, rows, cols = pair_bias.shape
    paired = (
        lax.axis_size("row") == 2
        and lax.axis_size("col") == 4
        and heads == HEADS
        and rows == single.shape[0]
        and 2 * cols == rows
        and cols % 128 == 0
    )
    plan = paired_plan if paired else general_plan
    return plan(single, pair_bias, *rest)


def solution(mesh):
    return jax.shard_map(
        on_device,
        mesh=mesh,
        in_specs=(
            P(("sample", "row"), None),
            P("sample", "row", "col"),
            P("sample"),
            P(),
            P(),
            P(),
            P(),
            P(),
            P(),
            P(None, "col"),
        ),
        out_specs=P(("sample", "row"), "col"),
        check_vma=False,
    )
```

```python
import math

import jax
import jax.numpy as jnp
from jax import lax
from jax.experimental import pallas as pl
from jax.experimental.pallas import tpu as pltpu
from jax.sharding import PartitionSpec as P

D = 384
HEADS = 16
EPS = 1e-05
HEAD_DIM = D // HEADS
SCALE = 1.0 / math.sqrt(HEAD_DIM)
NT = (((1,), (1,)), ((), ()))
F32 = jnp.float32
BF16 = jnp.bfloat16
PAD = 16
AHEAD = 8
CHUNK = 256
BAR_HI = -999424.0
BAR_LO = -576.0


def layer_norm(single, norm_gain):
    values_f32 = single.astype(jnp.float32)
    row_mean = jnp.mean(values_f32, axis=1, keepdims=True)
    centered = values_f32 - row_mean
    row_var = jnp.mean(centered * centered, axis=1, keepdims=True)
    return (centered * lax.rsqrt(row_var + EPS) * norm_gain).astype(jnp.bfloat16)


def attend(query_rows, key_rows, value_rows, bias_block, mask_cols):
    row_count = query_rows.shape[0]
    col_count = key_rows.shape[0]
    query_heads = query_rows.reshape(row_count, HEADS, -1)
    key_heads = key_rows.reshape(col_count, HEADS, -1)
    value_heads = value_rows.reshape(col_count, HEADS, -1)
    logits = jnp.einsum("qhd,khd->hqk", query_heads, key_heads, preferred_element_type=jnp.float32)
    mask_term = (mask_cols.astype(jnp.float32) - 1.0) * 1000000.0
    logits = logits + bias_block.astype(jnp.float32) + mask_term[None, None, :]
    row_peak = jnp.max(logits, axis=2)
    exp_scores = jnp.exp(logits - row_peak[:, :, None])
    row_total = jnp.sum(exp_scores, axis=2)
    weighted = jnp.einsum(
        "hqk,khd->qhd",
        exp_scores.astype(jnp.bfloat16),
        value_heads,
        preferred_element_type=jnp.float32,
    )
    return (row_total.T, weighted.reshape(row_count, -1))


def general_plan(
    single, pair_bias, token_mask, norm_gain, w_query, query_bias, w_key, w_value, w_gate, w_out
):
    tok_rows = single.shape[0]
    col_total = lax.axis_size("col")
    out_width = w_out.shape[1]
    col_pos = lax.axis_index("col")
    normed = layer_norm(single, norm_gain)
    query = (
        (jnp.dot(normed, w_query, preferred_element_type=jnp.float32) + query_bias) * SCALE
    ).astype(jnp.bfloat16)
    gate_act = jax.nn.sigmoid(jnp.dot(normed, w_gate, preferred_element_type=jnp.float32))
    single_cols = lax.dynamic_slice_in_dim(single, col_pos * out_width, out_width, 1).astype(
        jnp.float32
    )
    key_local = jnp.dot(normed, w_key, preferred_element_type=jnp.float32).astype(jnp.bfloat16)
    value_local = jnp.dot(normed, w_value, preferred_element_type=jnp.float32).astype(jnp.bfloat16)
    key_rows = lax.all_gather(key_local, "row", axis=0, tiled=True)
    value_rows = lax.all_gather(value_local, "row", axis=0, tiled=True)
    sub_rows = tok_rows // col_total
    query_start = col_pos * sub_rows
    bias_panel = lax.all_to_all(pair_bias, "col", split_axis=1, concat_axis=2, tiled=True)
    query_part = lax.dynamic_slice_in_dim(query, query_start, sub_rows, 0)
    gate_part = lax.dynamic_slice_in_dim(gate_act, query_start, sub_rows, 0)
    row_total, weighted = attend(query_part, key_rows, value_rows, bias_panel, token_mask)
    attended = weighted / jnp.repeat(row_total, HEAD_DIM, axis=1)
    gated_part = (gate_part * attended).astype(jnp.bfloat16)
    gated_all = lax.all_gather(gated_part, "col", axis=0, tiled=True)
    return single_cols + jnp.dot(gated_all, w_out, preferred_element_type=jnp.float32)


def place():
    col = lax.axis_index("col")
    row = lax.axis_index("row")
    chip = col // 2
    core = col % 2
    half = (chip + core) % 2
    return row, col, chip, core, half


def prepare_kernel(
    single_hbm, gain_hbm, mask_hbm, wq_hbm, bq_hbm, wk_hbm, wv_hbm, wg_hbm, wo_hbm,
    q_ref, gate_ref, wkv_ref, wo_own_ref, wo_oth_ref, res_ref, gain_out_ref, bar_ref,
    single_ref, gain_ref, mask_ref, wq_ref, bq_ref, wk_ref, wv_ref, wg_ref, wo_ref, tmp_ref, sems,
):
    _, col, chip, core, half = place()
    sources = (single_hbm, gain_hbm, wq_hbm, bq_hbm, wg_hbm, wk_hbm, wv_hbm, wo_hbm, mask_hbm)
    targets = (single_ref, gain_ref, wq_ref, bq_ref, wg_ref, wk_ref, wv_ref, wo_ref, mask_ref)
    copies = [
        pltpu.make_async_copy(src, dst, sems.at[i])
        for i, (src, dst) in enumerate(zip(sources, targets))
    ]
    for copy in copies:
        copy.start()
    hd = D // 2
    width = wo_ref.shape[0]
    n = single_ref.shape[0]
    blk = n // 2
    copies[0].wait()
    copies[1].wait()
    gain_out_ref[...] = gain_ref[...]
    x = single_ref[...].astype(F32)
    tmp_ref[:, :n] = x.T
    res_ref[...] = tmp_ref[pl.ds(pl.multiple_of(col * width, 8), width), :n]
    normed = layer_norm(single_ref[...], gain_ref[...][None, :])
    copies[2].wait()
    copies[3].wait()
    query = (jnp.dot(normed, wq_ref[...], preferred_element_type=F32) + bq_ref[...][None, :]) * SCALE
    query = jnp.where(half == 0, query[:, :hd], query[:, hd:])
    query = jnp.concatenate([query, jnp.ones((n, PAD), F32)], axis=1)
    feature = lax.broadcasted_iota(jnp.int32, query.shape, 1)
    bar_rows = (feature == hd) | (feature == hd + 1)
    for h in range(q_ref.shape[0]):
        lo = h * HEAD_DIM
        kept = ((feature >= lo) & (feature < lo + HEAD_DIM)) | bar_rows
        q_ref[h] = jnp.where(kept, query, 0.0).astype(BF16)
    copies[4].wait()
    gate = jnp.dot(normed, wg_ref[...], preferred_element_type=F32)
    tmp_ref[:, :n] = gate.T
    gate_ref[...] = jax.nn.sigmoid(tmp_ref[pl.ds(pl.multiple_of(half * hd, 8), hd), :n])
    copies[5].wait()
    tmp_ref[...] = wk_ref[...].astype(F32).T
    wkv_ref[:hd, :] = tmp_ref[pl.ds(pl.multiple_of(half * hd, 8), hd), :].astype(BF16)
    copies[6].wait()
    tmp_ref[...] = wv_ref[...].astype(F32).T
    wkv_ref[hd:, :] = tmp_ref[pl.ds(pl.multiple_of(half * hd, 8), hd), :].astype(BF16)
    copies[7].wait()
    wo = wo_ref[...].astype(F32)
    wo_own_ref[...] = jnp.where(half == 0, wo[:, :hd], wo[:, hd:]).astype(BF16)
    wo_oth_ref[...] = jnp.where(half == 0, wo[:, hd:], wo[:, :hd]).astype(BF16)
    copies[8].wait()
    base = chip * n
    first = pl.multiple_of(base + core * blk, blk)
    second = pl.multiple_of(base + (1 - core) * blk, blk)
    masked = jnp.concatenate([mask_ref[:, pl.ds(first, blk)], mask_ref[:, pl.ds(second, blk)]], axis=1)
    masked = 1.0 - masked.astype(F32)
    pad_row = lax.broadcasted_iota(jnp.int32, (PAD, n), 0)
    level = jnp.where(pad_row == 0, BAR_HI, jnp.where(pad_row == 1, BAR_LO, 0.0))
    bar_ref[...] = (level * masked).astype(BF16)


def widen_kernel(own_ref, other_ref, out_ref):
    _, _, _, _, half = place()
    heads, _, n_k = out_ref.shape
    for h in range(heads):
        out_ref[h, :, : n_k // 2] = own_ref[half * heads + h].astype(F32)
        out_ref[h, :, n_k // 2 :] = other_ref[half * heads + h].astype(F32)


def partial_kernel(
    recv_ref, own_ref, gain_ref, wkv_ref, q_ref, bias_ref, bar_ref,
    send_ref, att_ref, lse_ref,
):
    row, _, chip, core, _ = place()
    hd = D // 2
    heads = HEADS // 2
    n_q = q_ref.shape[1]
    n_k = recv_ref.shape[0]
    blk = n_k // 2
    first = pl.multiple_of(core * blk, blk)
    second = pl.multiple_of((1 - core) * blk, blk)

    local = chip == row
    block_a = jnp.where(local, own_ref[pl.ds(first, blk), :], recv_ref[pl.ds(first, blk), :])
    block_b = jnp.where(local, own_ref[pl.ds(second, blk), :], recv_ref[pl.ds(second, blk), :])
    gain = gain_ref[...][None, :]
    parts = [layer_norm(block, gain) for block in (block_a, block_b)]
    normed = jnp.concatenate(parts, axis=0)
    k_t = lax.dot_general(wkv_ref[:hd, :], normed, NT, preferred_element_type=F32)
    v_t = lax.dot_general(wkv_ref[hd:, :], normed, NT, preferred_element_type=F32)
    key_t = jnp.concatenate([k_t.astype(BF16), bar_ref[...]], axis=0)
    lane = lax.broadcasted_iota(jnp.int32, (n_q, 128), 1)
    peaks = jnp.zeros((n_q, 128), F32)
    ones = jnp.ones((8, n_k), F32)
    sums = []

    def logits_of(task):
        h, start = task
        return jnp.dot(q_ref[h, start : start + CHUNK, :], key_t, preferred_element_type=F32)

    tasks = [(h, start) for h in range(heads) for start in range(0, n_q, CHUNK)]
    ready = [logits_of(task) for task in tasks[:AHEAD]]
    probs, tops = [], []
    for i, (h, start) in enumerate(tasks):
        lo = h * HEAD_DIM
        rows = slice(start, start + CHUNK)
        logits = ready.pop(0)
        if i + AHEAD < len(tasks):
            ready.append(logits_of(tasks[i + AHEAD]))
        la = logits[:, :blk] + bias_ref[h, rows, :blk]
        lb = logits[:, blk:] + bias_ref[h, rows, blk:]
        peak = jnp.max(jnp.maximum(la, lb), axis=1, keepdims=True)
        probs.append(jnp.concatenate([jnp.exp(la - peak), jnp.exp(lb - peak)], axis=1).astype(BF16))
        tops.append(peak)
        if start + CHUNK < n_q:
            continue
        value = jnp.concatenate([v_t[lo : lo + HEAD_DIM], ones], axis=0).astype(BF16)
        out = lax.dot_general(
            value, jnp.concatenate(probs, axis=0), NT, preferred_element_type=F32
        )
        total = out[HEAD_DIM : HEAD_DIM + 1]
        att = out[:HEAD_DIM] / total
        att_ref[lo : lo + HEAD_DIM, :] = att
        send_ref[lo : lo + HEAD_DIM, :] = att.astype(BF16)
        sums.append(total)
        peaks = jnp.where(lane == h, jnp.concatenate(tops, axis=0), peaks)
        probs, tops = [], []
    lse = peaks.T[:heads] + jnp.log(jnp.concatenate(sums, axis=0))
    lse_ref[...] = lse
    hi = lse.astype(BF16)
    rest = lse - hi.astype(F32)
    mid = rest.astype(BF16)
    low = (rest - mid.astype(F32)).astype(BF16)
    send_ref[hd : hd + heads, :] = hi
    send_ref[hd + heads : hd + 2 * heads, :] = mid
    send_ref[hd + 2 * heads :, :] = low


def merge_kernel(recv_ref, att_ref, lse_ref, gate_ref, gated_ref):
    hd = D // 2
    heads = HEADS // 2
    parts = recv_ref[hd:, :].astype(F32)
    other = parts[:heads] + parts[heads : 2 * heads] + parts[2 * heads :]
    own = lse_ref[...]
    top = jnp.maximum(own, other)
    w_own = jnp.exp(own - top)
    w_oth = jnp.exp(other - top)
    inv = 1.0 / (w_own + w_oth)
    w_own = w_own * inv
    w_oth = w_oth * inv
    pieces = []
    for h in range(heads):
        rows = slice(h * HEAD_DIM, (h + 1) * HEAD_DIM)
        att = w_own[h : h + 1] * att_ref[rows, :] + w_oth[h : h + 1] * recv_ref[rows, :].astype(F32)
        pieces.append(gate_ref[rows, :] * att)
    gated_ref[...] = jnp.concatenate(pieces, axis=0).astype(BF16)


def own_project_kernel(own_ref, wo_own_ref, res_ref, acc_ref):
    acc_ref[...] = res_ref[...] + jnp.dot(wo_own_ref[...], own_ref[...], preferred_element_type=F32)


def project_kernel(acc_ref, oth_ref, wo_oth_ref, out_hbm, buf_ref, sems):
    step = buf_ref.shape[0] // 2
    copies = []
    for i in range(2):
        rows = slice(i * step, (i + 1) * step)
        buf_ref[rows, :] = acc_ref[rows, :] + jnp.dot(
            wo_oth_ref[rows, :], oth_ref[...], preferred_element_type=F32
        )
        copy = pltpu.make_async_copy(buf_ref.at[rows, :], out_hbm.at[rows, :], sems.at[i])
        copy.start()
        copies.append(copy)
    for copy in copies:
        copy.wait()


def call(kernel, outs, args, scratch=(), flops=0, trans=0, fetch=False, out_space=pltpu.VMEM):
    vmem = pl.BlockSpec(memory_space=pltpu.VMEM)
    source = pl.BlockSpec(memory_space=pltpu.HBM) if fetch else vmem
    if fetch:
        args = [pltpu.with_memory_space_constraint(a, pltpu.HBM) for a in args]
    nbytes = sum(math.prod(a.shape) * a.dtype.itemsize for a in (*args, *outs))
    return pl.pallas_call(
        kernel,
        out_shape=tuple(outs),
        in_specs=[source] * len(args),
        out_specs=tuple([pl.BlockSpec(memory_space=out_space)] * len(outs)),
        scratch_shapes=list(scratch),
        cost_estimate=pl.CostEstimate(flops=flops, bytes_accessed=nbytes, transcendentals=trans),
        compiler_params=pltpu.CompilerParams(vmem_limit_bytes=16 << 20),
    )(*args)


def paired_plan(
    single, pair_bias, token_mask, norm_gain, w_query, query_bias, w_key, w_value, w_gate, w_out
):
    n = single.shape[0]
    heads, _, _ = pair_bias.shape
    width = w_out.shape[1]
    hd = D // 2
    half_heads = heads // 2
    shape = jax.ShapeDtypeStruct
    swap_row = [(r * 4 + c, (1 - r) * 4 + (c ^ 1)) for r in range(2) for c in range(4)]
    swap_core = [(c, c ^ 1) for c in range(4)]
    swap_chip = [(c, c ^ 3) for c in range(4)]

    single_in = lax.ppermute(single, ("row", "col"), swap_row)
    bias_in = lax.ppermute(pair_bias, "col", swap_core)
    fetched = (
        single, norm_gain, token_mask.reshape(1, -1), w_query, query_bias, w_key, w_value, w_gate, w_out.T,
    )
    query, gate, wkv, wo_own, wo_oth, res, gain, bar = call(
        prepare_kernel,
        [
            shape((half_heads, n, hd + PAD), BF16),
            shape((hd, n), F32),
            shape((D, D), BF16),
            shape((width, hd), BF16),
            shape((width, hd), BF16),
            shape((width, n), F32),
            shape((D,), F32),
            shape((PAD, n), BF16),
        ],
        fetched,
        [
            *(pltpu.VMEM(a.shape, a.dtype) for a in fetched),
            pltpu.VMEM((D, D), F32),
            pltpu.SemaphoreType.DMA((len(fetched),)),
        ],
        flops=4 * n * D * D,
        fetch=True,
    )
    (bias,) = call(
        widen_kernel, [shape((half_heads, n, n), F32)], (pair_bias, bias_in), flops=half_heads * n * n
    )
    send, att, lse = call(
        partial_kernel,
        [
            shape((hd + 3 * half_heads, n), BF16),
            shape((hd, n), F32),
            shape((half_heads, n), F32),
        ],
        (single_in, single, gain, wkv, query, bias, bar),
        flops=4 * n * D * D,
        trans=half_heads * n * n,
    )
    recv = lax.ppermute(send, "col", swap_chip)
    (gated_own,) = call(merge_kernel, [shape((hd, n), BF16)], (recv, att, lse, gate), flops=n * D)
    gated_oth = lax.ppermute(gated_own, "col", swap_core)
    (acc,) = call(
        own_project_kernel,
        [shape((width, n), F32)],
        (gated_own, wo_own, res),
        flops=n * D * width,
    )
    (out,) = call(
        project_kernel,
        [shape((width, n), F32)],
        (acc, gated_oth, wo_oth),
        [pltpu.VMEM((width, n), F32), pltpu.SemaphoreType.DMA((2,))],
        flops=n * D * width,
        out_space=pltpu.HBM,
    )
    return out.T


def on_device(single, pair_bias, *rest):
    heads, rows, cols = pair_bias.shape
    paired = (
        lax.axis_size("row") == 2
        and lax.axis_size("col") == 4
        and heads == HEADS
        and rows == single.shape[0]
        and 2 * cols == rows
        and cols % 128 == 0
    )
    plan = paired_plan if paired else general_plan
    return plan(single, pair_bias, *rest)


def solution(mesh):
    return jax.shard_map(
        on_device,
        mesh=mesh,
        in_specs=(
            P(("sample", "row"), None),
            P("sample", "row", "col"),
            P("sample"),
            P(),
            P(),
            P(),
            P(),
            P(),
            P(),
            P(None, "col"),
        ),
        out_specs=P(("sample", "row"), "col"),
        check_vma=False,
    )
```
